512 devices in a mesh: seq: 64 (over z, y), head: 8 (over x, core).
Axes of the slice: x: 4, y: 4, z: 16, core: 2. Of those that a mesh axis runs over, the one named last changes fastest.
Arguments:
- queries: bfloat16 [131072, 2048], P(('seq', 'head')), may hold values from -12 to 12
- key_vectors: bfloat16 [131072, 2048], P(('seq', 'head')), may hold values from -6 to 6
- value_vectors: bfloat16 [131072, 2048], P(('seq', 'head')), may hold values from -6 to 6
- key_blocks: int32 [1024, 14], P('seq'), may hold values from -1 to 1023, as said below
Outputs:
- context: bfloat16 [131072, 2048], P(('seq', 'head'))
The draws below stay inside these ranges and needn't reach their ends.
Inputs may be any that keep to these rules, and one draw needn't show every extreme that they name: `key_blocks`: row b lists key blocks of query block b. Slots 0 to 9, in falling order: b itself, then 10 - 1 distinct blocks among b - 15 to b - 1, written as -1 where the block number would be negative. Slot 10 + i holds the i-th global block where that block is at most b - 16, else -1. The 4 global blocks are the same for all rows, distinct and rising, the first is 0, and all lie below 1008.
All inputs are finite; a program needn't handle non-finite values.
Results may differ from the reference program's by a relative error of at most 0.0032.
Values may be sent and summed in bfloat16 or wider, within the bound.
No kernel may reach another device: no remote copies, remote signals or barrier semaphores. Data moves between devices by JAX's collectives and lax.ppermute only.
A program may use at most 64 MiB of HBM per device.

```python
import math
import jax
import jax.numpy as jnp
from jax import lax

HEAD_DIM = 128
BLOCK = 128
WIN = 16
WSEL = 10
GLOBALS = 4
WIDTH = 2048
NQB = 1024
SEQ = 131072


def draw_queries(key, part):
    result = jnp.clip(2.5 * jax.random.normal(jax.random.fold_in(key, 41), (SEQ, WIDTH), jnp.float32), -12.0, 12.0)
    return result.astype(jnp.bfloat16)


def draw_key_vectors(key, part):
    result = jnp.clip(jax.random.normal(jax.random.fold_in(key, 51), (SEQ, WIDTH), jnp.float32), -6.0, 6.0)
    return result.astype(jnp.bfloat16)


def draw_key_blocks(key, part):
    span_back = WIN - 1
    cand_count = NQB - WIN - 1
    glob_scores = jax.random.randint(jax.random.fold_in(key, 61), (cand_count,), 0, 65536) * cand_count + jnp.arange(cand_count, dtype=jnp.int32)
    glob_pick = jnp.sort(jnp.argsort(glob_scores)[:GLOBALS - 1].astype(jnp.int32) + 1)
    global_ids = jnp.concatenate((jnp.zeros((1,), jnp.int32), glob_pick))
    back_scores = jax.random.randint(jax.random.fold_in(key, 67), (NQB, span_back), 0, 65536) * span_back + jnp.arange(span_back, dtype=jnp.int32)[None, :]
    offsets = jnp.argsort(back_scores, axis=1)[:, :WSEL - 1].astype(jnp.int32) + 1
    offsets = jnp.sort(jnp.concatenate((jnp.zeros((NQB, 1), jnp.int32), offsets), 1), axis=1)
    row_ids = jnp.arange(NQB, dtype=jnp.int32)[:, None]
    window_ids = row_ids - offsets
    window_ids = jnp.where(window_ids >= 0, window_ids, -1)
    global_cols = jnp.where(global_ids[None, :] <= row_ids - WIN, global_ids[None, :], -1)
    return jnp.concatenate((window_ids, global_cols), 1).astype(jnp.int32)


def shard_levels(stream_key, extent, cuts, smallest, top_value):
    factor_of = 1.0
    for axis_at, blocks in cuts:
        heights = jax.random.uniform(jax.random.fold_in(jax.random.fold_in(stream_key, 6), axis_at), (blocks,), jnp.float32, smallest / len(cuts), top_value / len(cuts))
        factor_of = factor_of * jnp.repeat(jnp.exp(heights), extent[axis_at] // blocks).reshape((-1,) + (1,) * (len(extent) - 1 - axis_at))
    return factor_of


def scatter_about(rng, shape, scale, most, shards=(), held_as=jnp.bfloat16):
    factor_of = shard_levels(rng, shape, shards, -0.22, 0.18) if shards else 1.0
    entries = jax.random.normal(rng, shape, jnp.float32) * scale * factor_of
    return jnp.minimum(jnp.maximum(entries, -most), most).astype(held_as)


def setup_inputs(seed: int = 0) -> dict:
    streams_of = jax.random.split(jax.random.key(seed), 5)
    queries = draw_queries(jax.random.fold_in(streams_of[4], 71), 0)
    key_vectors = draw_key_vectors(jax.random.fold_in(streams_of[4], 71), 0)
    value_vectors = scatter_about(streams_of[2], (SEQ, WIDTH), 1.0, 6.0, ((0, 512),))
    key_blocks = draw_key_blocks(jax.random.fold_in(streams_of[4], 71), 0)
    return dict(queries=queries, key_vectors=key_vectors, value_vectors=value_vectors, key_blocks=key_blocks)


def attend_block(query_block, key_rows, value_rows, block_ids, block_pos, causal):
    slot_count = block_ids.shape[0]
    head_count = query_block.shape[1] // HEAD_DIM
    query_heads = query_block.reshape(BLOCK, head_count, HEAD_DIM).astype(jnp.float32)
    key_heads = key_rows.reshape(slot_count, BLOCK, head_count, HEAD_DIM).astype(jnp.float32)
    value_heads = value_rows.reshape(slot_count, BLOCK, head_count, HEAD_DIM).astype(jnp.float32)
    scores = jnp.einsum('thd,juhd->htju', query_heads, key_heads) * (1.0 / math.sqrt(HEAD_DIM))
    allowed = (block_ids >= 0)[None, :, None] & ((block_ids < block_pos)[None, :, None] | causal[:, None, :])
    scores = jnp.where(allowed[None], scores, -1e+30)
    row_max = lax.optimization_barrier(jnp.max(scores, axis=(2, 3), keepdims=True))
    weight = jnp.where(allowed[None], jnp.exp(scores - row_max), 0.0)
    denom_sum = lax.optimization_barrier(jnp.sum(weight, axis=(2, 3)))
    weight_low = lax.optimization_barrier(weight.astype(jnp.bfloat16))
    mixed_sum = jnp.einsum('htju,juhd->thd', weight_low.astype(jnp.float32), value_heads)
    return (mixed_sum / jnp.transpose(denom_sum)[:, :, None]).astype(jnp.bfloat16).reshape(BLOCK, head_count * HEAD_DIM)

def reference(queries, key_vectors, value_vectors, key_blocks):
    block_total = key_blocks.shape[0]
    full_width = queries.shape[1]
    query_tiles = queries.reshape(block_total, BLOCK, full_width)
    key_tiles = key_vectors.reshape(block_total, BLOCK, full_width)
    value_tiles = value_vectors.reshape(block_total, BLOCK, full_width)
    causal = lax.broadcasted_iota(jnp.int32, (BLOCK, BLOCK), 0) >= lax.broadcasted_iota(jnp.int32, (BLOCK, BLOCK), 1)

    def one_block(block_item):
        query_block, block_ids, block_pos = block_item
        safe_ids = jnp.maximum(block_ids, 0).astype(jnp.int32)
        return attend_block(query_block, jnp.take(key_tiles, safe_ids, axis=0), jnp.take(value_tiles, safe_ids, axis=0), block_ids, block_pos, causal)
    context = lax.map(one_block, (query_tiles, key_blocks, jnp.arange(block_total, dtype=jnp.int32)))
    return context.reshape(queries.shape[0], full_width)
```

```python
import functools
import math

import jax
import jax.numpy as jnp
from jax import lax
from jax.experimental import pallas as pl
from jax.experimental.pallas import tpu as pltpu
from jax.sharding import Mesh
from jax.sharding import PartitionSpec as P

HEAD_DIM = 128
BLOCK = 128
WIN = 16
WSEL = 10
GLOBALS = 4
SLOTS = WSEL + GLOBALS
HEADS = 16
PLANE = 64
FACTOR = math.log2(math.e) / math.sqrt(HEAD_DIM)
UNROLL = 4
PLANE_AXES = ("y", "x", "core")


def pick_kernel(ids, first, kinds, out):
    for slot in range(GLOBALS):
        place = ids[slot] - first[0]
        held = (place >= 0) & (place < PLANE)
        block = kinds[jnp.where(held, place, 0)]
        out[slot] = jnp.where(held, block, jnp.zeros_like(block))


def pick_globals(ids, first, kinds):
    scalars = pl.BlockSpec(memory_space=pltpu.SMEM)
    whole = pl.BlockSpec(memory_space=pltpu.VMEM)
    return pl.pallas_call(
        pick_kernel,
        out_shape=jax.ShapeDtypeStruct((GLOBALS, BLOCK, HEAD_DIM), jnp.bfloat16),
        in_specs=[scalars, scalars, whole],
        out_specs=whole,
        name="pick_globals",
    )(ids, first, kinds)


def attend_kernel(
    where, rows, query, own, other, halo_own, halo_other, global_own, global_other,
    out, keys, values, scores, weights, sems,
):
    core = where[0]
    first = where[1]

    def fill(own_to, other_to):
        copies = [
            (own, own_to.at[pl.ds(0, PLANE)]),
            (other, other_to.at[pl.ds(0, PLANE)]),
            (halo_own, own_to.at[pl.ds(PLANE, WIN)]),
            (halo_other, other_to.at[pl.ds(PLANE, WIN)]),
            (global_own, own_to.at[pl.ds(PLANE + WIN, GLOBALS)]),
            (global_other, other_to.at[pl.ds(PLANE + WIN, GLOBALS)]),
        ]
        started = [
            pltpu.make_async_copy(source, target, sems.at[at])
            for at, (source, target) in enumerate(copies)
        ]
        for copy in started:
            copy.start()
        for copy in started:
            copy.wait()

    @pl.when(core == 0)
    def _():
        fill(keys, values)

    @pl.when(core != 0)
    def _():
        fill(values, keys)

    causal = lax.broadcasted_iota(jnp.int32, (BLOCK, BLOCK), 0) >= lax.broadcasted_iota(
        jnp.int32, (BLOCK, BLOCK), 1
    )

    def attend_block(at, lane):
        row = 2 * at + core
        block_query = query[at]
        places, listed = [], []
        for slot in range(SLOTS):
            block_id = rows[row, slot]
            if slot < WSEL:
                offset = block_id - first
                place = jnp.where(offset >= 0, offset, offset + PLANE + WIN)
            else:
                place = PLANE + WIN + slot - WSEL
            listed.append(block_id >= 0)
            places.append(jnp.where(block_id >= 0, place, 0))
        highest = None
        for slot in range(0, SLOTS, 2):
            pair = jnp.concatenate([keys[places[slot]], keys[places[slot + 1]]], axis=0)
            both = lax.dot_general(
                block_query, pair, (((1,), (1,)), ((), ())), preferred_element_type=jnp.float32
            )
            for part in range(2):
                score = both[:, part * BLOCK : (part + 1) * BLOCK]
                allowed = causal if slot + part == 0 else listed[slot + part]
                score = jnp.where(allowed, score, -1e30)
                scores[lane, slot + part] = score
                highest = score if highest is None else jnp.maximum(highest, score)
        row_max = jnp.max(highest, axis=1, keepdims=True) * FACTOR
        row_max = jnp.broadcast_to(row_max, (BLOCK, BLOCK))
        total = None
        for slot in range(SLOTS):
            weight = jnp.exp2(scores[lane, slot] * FACTOR - row_max)
            total = weight if total is None else total + weight
            weights[lane, :, slot * BLOCK : (slot + 1) * BLOCK] = weight.astype(jnp.bfloat16)
        mixed = None
        for slot in range(0, SLOTS, 2):
            pair = jnp.concatenate([values[places[slot]], values[places[slot + 1]]], axis=0)
            term = jnp.dot(
                weights[lane, :, slot * BLOCK : (slot + 2) * BLOCK],
                pair,
                preferred_element_type=jnp.float32,
            )
            mixed = term if mixed is None else mixed + term
        denom = jnp.sum(total, axis=1, keepdims=True)
        out[at] = (mixed / denom).astype(jnp.bfloat16)

    def step(at, carry):
        for lane in range(UNROLL):
            attend_block(at * UNROLL + lane, lane)
        return carry

    lax.fori_loop(0, query.shape[0] // UNROLL, step, 0)


def attend(where, rows, query, own, other, halo_own, halo_other, global_own, global_other):
    scalars = pl.BlockSpec(memory_space=pltpu.SMEM)
    whole = pl.BlockSpec(memory_space=pltpu.VMEM)
    left = pl.BlockSpec(memory_space=pl.ANY)
    span = PLANE + WIN + GLOBALS
    pairs = query.shape[0] * SLOTS * BLOCK * BLOCK
    return pl.pallas_call(
        attend_kernel,
        out_shape=jax.ShapeDtypeStruct(query.shape, jnp.bfloat16),
        in_specs=[scalars, scalars, whole] + [left] * 6,
        out_specs=whole,
        scratch_shapes=[
            pltpu.VMEM((span, BLOCK, HEAD_DIM), jnp.bfloat16),
            pltpu.VMEM((span, BLOCK, HEAD_DIM), jnp.bfloat16),
            pltpu.VMEM((UNROLL, SLOTS, BLOCK, BLOCK), jnp.float32),
            pltpu.VMEM((UNROLL, BLOCK, SLOTS * BLOCK), jnp.bfloat16),
            pltpu.SemaphoreType.DMA((6,)),
        ],
        compiler_params=pltpu.CompilerParams(vmem_limit_bytes=40 << 20),
        cost_estimate=pl.CostEstimate(
            flops=4 * pairs * HEAD_DIM, bytes_accessed=8 << 20, transcendentals=pairs
        ),
        name="attend",
    )(where, rows, query, own, other, halo_own, halo_other, global_own, global_other)


def swapped(value):
    return lax.ppermute(value, "core", [(0, 1), (1, 0)])


def shards(queries, key_vectors, value_vectors, key_blocks):
    depth = lax.axis_size("z")
    breadth = lax.axis_size("y")
    up = [(at, at + 1) for at in range(depth - 1)]
    down = [(at + 1, at) for at in range(depth - 1)]
    core = lax.axis_index("core")
    first = lax.axis_index("z") * PLANE

    tokens = queries.shape[0]
    kinds = jnp.stack(
        [
            jnp.swapaxes(array.reshape(tokens, HEADS, HEAD_DIM), 0, 1)
            for array in (key_vectors, value_vectors)
        ],
        axis=1,
    ).reshape(2 * HEADS, tokens, HEAD_DIM)
    own = lax.all_to_all(kinds, PLANE_AXES, 0, 0, tiled=True).reshape(PLANE, BLOCK, HEAD_DIM)

    turned = [key_blocks] + [
        lax.ppermute(key_blocks, "y", [(at, (at + step) % breadth) for at in range(breadth)])
        for step in range(1, breadth)
    ]
    here = lax.axis_index("y")
    rows = jnp.stack(turned)[(here - jnp.arange(breadth)) % breadth].reshape(PLANE, SLOTS)
    above = lax.ppermute(key_blocks[-1, WSEL:], "z", down)
    ids = jnp.maximum(rows[-1, WSEL:], above)

    query = lax.all_to_all(
        jnp.transpose(
            queries.reshape(2, BLOCK, HEADS, HEAD_DIM), (2, 0, 1, 3)
        ).reshape(2 * HEADS, BLOCK, HEAD_DIM),
        PLANE_AXES, 0, 0, tiled=True,
    )

    other = swapped(own)
    halo_own = lax.ppermute(own[PLANE - WIN :], "z", up)
    halo_other = swapped(halo_own)

    part = pick_globals(ids, first[None], own).reshape(depth, -1, HEAD_DIM)
    pieces = lax.all_to_all(part, "z", 0, 0, tiled=True)
    summed = jnp.sum(pieces.astype(jnp.float32), axis=0, keepdims=True).astype(jnp.bfloat16)
    global_own = lax.all_to_all(
        jnp.broadcast_to(summed, part.shape), "z", 0, 0, tiled=True
    ).reshape(GLOBALS, BLOCK, HEAD_DIM)
    global_other = swapped(global_own)

    context = attend(
        jnp.stack([core, first]), rows, query,
        own, other, halo_own, halo_other, global_own, global_other,
    )
    back = lax.all_to_all(context, PLANE_AXES, 0, 0, tiled=True)
    return jnp.transpose(
        back.reshape(HEADS, 2, BLOCK, HEAD_DIM), (1, 2, 0, 3)
    ).reshape(tokens, HEADS * HEAD_DIM)


def solution(mesh):
    fine = Mesh(mesh.devices.reshape(-1, 4, 4, 2), ("z",) + PLANE_AXES)
    tokens = P(("z",) + PLANE_AXES, None)
    return jax.shard_map(
        shards,
        mesh=fine,
        in_specs=(tokens, tokens, tokens, P(("z", "y"), None)),
        out_specs=tokens,
        check_vma=False,
    )
```

```python
import functools
import math

import jax
import jax.numpy as jnp
from jax import lax
from jax.experimental import pallas as pl
from jax.experimental.pallas import tpu as pltpu
from jax.sharding import Mesh
from jax.sharding import PartitionSpec as P

HEAD_DIM = 128
BLOCK = 128
WIN = 16
WSEL = 10
GLOBALS = 4
SLOTS = WSEL + GLOBALS
HEADS = 16
PLANE = 64
CHUNK = 16
FACTOR = math.log2(math.e) / math.sqrt(HEAD_DIM)
UNROLL = 4
PLANE_AXES = ("y", "x", "core")

SCALARS = pl.BlockSpec(memory_space=pltpu.SMEM)
WHOLE = pl.BlockSpec(memory_space=pltpu.VMEM)
LEFT = pl.BlockSpec(memory_space=pl.ANY)
BF16_TILE = jax.ShapeDtypeStruct((BLOCK, HEAD_DIM), jnp.bfloat16)


def pick_kernel(where, rows, above, kinds, *refs):
    outs, (buffer, sems) = refs[:GLOBALS], refs[GLOBALS:]
    first, turn = where[1], where[2]
    last = (where[3] + GLOBALS - PLANE // CHUNK + 1) % GLOBALS
    copies, present = [], []
    for step in range(GLOBALS):
        slot = (turn + step) % GLOBALS
        place = jnp.maximum(rows[last, CHUNK - 1, WSEL + slot], above[slot]) - first
        held = (place >= 0) & (place < PLANE)
        copies.append(
            pltpu.make_async_copy(
                kinds.at[jnp.where(held, place, 0)], buffer.at[step], sems.at[step]
            )
        )
        present.append(held)
    for copy in copies:
        copy.start()
    for step in range(GLOBALS):
        copies[step].wait()
        block = buffer[step]
        outs[step][...] = jnp.where(present[step], block, jnp.zeros_like(block))


def pick_globals(where, rows, above, kinds):
    return pl.pallas_call(
        pick_kernel,
        out_shape=[BF16_TILE] * GLOBALS,
        in_specs=[SCALARS, SCALARS, SCALARS, LEFT],
        out_specs=[WHOLE] * GLOBALS,
        scratch_shapes=[
            pltpu.VMEM((GLOBALS, BLOCK, HEAD_DIM), jnp.bfloat16),
            pltpu.SemaphoreType.DMA((GLOBALS,)),
        ],
        compiler_params=pltpu.CompilerParams(vmem_limit_bytes=20 << 20),
        name="pick_globals",
    )(where, rows, above, kinds)


def row_of(where, at):
    row = 2 * at + where[0]
    return (where[3] + GLOBALS - row // CHUNK) % GLOBALS, row % CHUNK


def window_kernel(start, low, high, with_halo, where, rows, query, own, other, *refs):
    if with_halo:
        halo_own, halo_other, *refs = refs
    out, out_max, out_sum, keys, values, scores, weights, sems = refs
    core, first = where[0], where[1]
    count = out.shape[0]
    chunks = (high - low) // CHUNK

    def copies(own_to, other_to, at):
        if at < chunks:
            source, target = pl.ds(low + at * CHUNK, CHUNK), pl.ds(at * CHUNK, CHUNK)
            yield pltpu.make_async_copy(own.at[source], own_to.at[target], sems.at[0, at])
            yield pltpu.make_async_copy(other.at[source], other_to.at[target], sems.at[1, at])
        else:
            target = pl.ds(at * CHUNK, WIN)
            yield pltpu.make_async_copy(halo_own, own_to.at[target], sems.at[0, at])
            yield pltpu.make_async_copy(halo_other, other_to.at[target], sems.at[1, at])

    parts = list(range(chunks)) + ([chunks] if with_halo else [])

    @pl.when(core == 0)
    def _():
        for part in parts:
            for copy in copies(keys, values, part):
                copy.start()

    @pl.when(core != 0)
    def _():
        for part in parts:
            for copy in copies(values, keys, part):
                copy.start()

    needed = {}
    for part in parts:
        step = 0
        if part < chunks:
            step = max(0, (low + part * CHUNK - 2 * start) // (2 * UNROLL))
        needed.setdefault(step, []).append(part)

    causal = lax.broadcasted_iota(jnp.int32, (BLOCK, BLOCK), 0) >= lax.broadcasted_iota(
        jnp.int32, (BLOCK, BLOCK), 1
    )

    def attend_block(at, lane):
        group, row = row_of(where, start + at)
        block_query = query[start + at]
        places, listed = [], []
        for slot in range(WSEL):
            block_id = rows[group, row, slot]
            place = block_id - first - low
            if with_halo:
                place = jnp.where(place >= 0, place, place + high + WIN)
            listed.append(block_id >= 0)
            places.append(jnp.where(block_id >= 0, place, 0))
        highest = None
        for slot in range(0, WSEL, 2):
            pair = jnp.concatenate([keys[places[slot]], keys[places[slot + 1]]], axis=0)
            both = lax.dot_general(
                block_query, pair, (((1,), (1,)), ((), ())), preferred_element_type=jnp.float32
            )
            for part in range(2):
                score = both[:, part * BLOCK : (part + 1) * BLOCK]
                if slot + part == 0:
                    score = jnp.where(causal, score, -1e30)
                elif with_halo:
                    score = jnp.where(listed[slot + part], score, -1e30)
                scores[lane, slot + part] = score
                highest = score if highest is None else jnp.maximum(highest, score)
        row_max = jnp.max(highest, axis=1, keepdims=True) * FACTOR
        row_max = jnp.broadcast_to(row_max, (BLOCK, BLOCK))
        out_max[at] = row_max
        total = None
        for slot in range(WSEL):
            weight = jnp.exp2(scores[lane, slot] * FACTOR - row_max)
            total = weight if total is None else total + weight
            weights[lane, :, slot * BLOCK : (slot + 1) * BLOCK] = weight.astype(jnp.bfloat16)
        out_sum[at] = total
        mixed = None
        for slot in range(0, WSEL, 2):
            pair = jnp.concatenate([values[places[slot]], values[places[slot + 1]]], axis=0)
            term = jnp.dot(
                weights[lane, :, slot * BLOCK : (slot + 2) * BLOCK],
                pair,
                preferred_element_type=jnp.float32,
            )
            mixed = term if mixed is None else mixed + term
        out[at] = mixed

    def step(at, carry):
        for when, needs in needed.items():

            @pl.when(at == when)
            def _(needs=needs):
                for part in needs:
                    for copy in copies(keys, values, part):
                        copy.wait()

        for lane in range(UNROLL):
            attend_block(at * UNROLL + lane, lane)
        return carry

    lax.fori_loop(0, count // UNROLL, step, 0)


def attend_window(start, count, low, high, where, rows, query, own, other, *halo):
    span = high - low + (WIN if halo else 0)
    sums = jax.ShapeDtypeStruct((count, BLOCK, HEAD_DIM), jnp.float32)
    pairs = count * WSEL * BLOCK * BLOCK
    return pl.pallas_call(
        functools.partial(window_kernel, start, low, high, bool(halo)),
        out_shape=[sums] * 3,
        in_specs=[SCALARS, SCALARS, WHOLE] + [LEFT] * (2 + len(halo)),
        out_specs=[WHOLE] * 3,
        scratch_shapes=[
            pltpu.VMEM((span, BLOCK, HEAD_DIM), jnp.bfloat16),
            pltpu.VMEM((span, BLOCK, HEAD_DIM), jnp.bfloat16),
            pltpu.VMEM((UNROLL, WSEL, BLOCK, BLOCK), jnp.float32),
            pltpu.VMEM((UNROLL, BLOCK, WSEL * BLOCK), jnp.bfloat16),
            pltpu.SemaphoreType.DMA((2, span // CHUNK)),
        ],
        compiler_params=pltpu.CompilerParams(vmem_limit_bytes=20 << 20),
        cost_estimate=pl.CostEstimate(
            flops=4 * pairs * HEAD_DIM, bytes_accessed=8 << 20, transcendentals=pairs
        ),
        name="attend_near" if halo else "attend_far",
    )(where, rows, query, own, other, *halo)


def global_kernel(
    where, rows, query, own, other, near_sum, near_max, near_total, far_sum, far_max, far_total,
    out, keys, values, weights, sems,
):
    core, turn = where[0], where[2]

    def copies(own_to, other_to):
        yield pltpu.make_async_copy(own, own_to, sems.at[0])
        yield pltpu.make_async_copy(other, other_to, sems.at[1])

    @pl.when(core == 0)
    def _():
        for copy in copies(keys, values):
            copy.start()

    @pl.when(core != 0)
    def _():
        for copy in copies(values, keys):
            copy.start()

    for copy in copies(keys, values):
        copy.wait()

    slots = [(turn + GLOBALS - step) % GLOBALS for step in range(GLOBALS)]

    def merge(at, of, lane, sums, maxima, totals):
        group, row = row_of(where, at)
        block_query = query[at]
        listed = [rows[group, row, WSEL + slot] >= 0 for slot in slots]
        held, highest = [], None
        for step in range(0, GLOBALS, 2):
            pair = jnp.concatenate([keys[step], keys[step + 1]], axis=0)
            both = lax.dot_general(
                block_query, pair, (((1,), (1,)), ((), ())), preferred_element_type=jnp.float32
            )
            for part in range(2):
                score = both[:, part * BLOCK : (part + 1) * BLOCK]
                score = jnp.where(listed[step + part], score, -1e30)
                held.append(score)
                highest = score if highest is None else jnp.maximum(highest, score)
        row_max = jnp.max(highest, axis=1, keepdims=True) * FACTOR
        window_max = maxima[of]
        row_max = jnp.maximum(jnp.broadcast_to(row_max, (BLOCK, BLOCK)), window_max)
        shrink = jnp.exp2(window_max - row_max)
        total = totals[of] * shrink
        for step in range(GLOBALS):
            weight = jnp.exp2(held[step] * FACTOR - row_max)
            total = total + weight
            weights[lane, :, step * BLOCK : (step + 1) * BLOCK] = weight.astype(jnp.bfloat16)
        mixed = sums[of] * shrink
        for step in range(0, GLOBALS, 2):
            pair = jnp.concatenate([values[step], values[step + 1]], axis=0)
            mixed = mixed + jnp.dot(
                weights[lane, :, step * BLOCK : (step + 2) * BLOCK],
                pair,
                preferred_element_type=jnp.float32,
            )
        denom = jnp.sum(total, axis=1, keepdims=True)
        out[at] = (mixed / denom).astype(jnp.bfloat16)

    split = near_sum.shape[0]

    def near(at, carry):
        for lane in range(UNROLL):
            merge(at * UNROLL + lane, at * UNROLL + lane, lane, near_sum, near_max, near_total)
        return carry

    def far(at, carry):
        for lane in range(UNROLL):
            of = at * UNROLL + lane
            merge(split + of, of, lane, far_sum, far_max, far_total)
        return carry

    lax.fori_loop(0, split // UNROLL, near, 0)
    lax.fori_loop(0, far_sum.shape[0] // UNROLL, far, 0)


def attend_global(where, rows, query, own, other, near, far):
    pairs = query.shape[0] * GLOBALS * BLOCK * BLOCK
    return pl.pallas_call(
        global_kernel,
        out_shape=jax.ShapeDtypeStruct(query.shape, jnp.bfloat16),
        in_specs=[SCALARS, SCALARS, WHOLE, LEFT, LEFT] + [WHOLE] * 6,
        out_specs=WHOLE,
        scratch_shapes=[
            pltpu.VMEM((GLOBALS, BLOCK, HEAD_DIM), jnp.bfloat16),
            pltpu.VMEM((GLOBALS, BLOCK, HEAD_DIM), jnp.bfloat16),
            pltpu.VMEM((UNROLL, BLOCK, GLOBALS * BLOCK), jnp.bfloat16),
            pltpu.SemaphoreType.DMA((2,)),
        ],
        compiler_params=pltpu.CompilerParams(vmem_limit_bytes=20 << 20),
        cost_estimate=pl.CostEstimate(
            flops=4 * pairs * HEAD_DIM, bytes_accessed=8 << 20, transcendentals=pairs
        ),
        name="attend_global",
    )(where, rows, query, own, other, *near, *far)


def swapped(value):
    return lax.ppermute(value, "core", [(0, 1), (1, 0)])


def added(*values):
    return sum(value.astype(jnp.float32) for value in values).astype(jnp.bfloat16)


def shards(queries, key_vectors, value_vectors, key_blocks):
    depth = lax.axis_size("z")
    breadth = lax.axis_size("y")
    up = [(at, at + 1) for at in range(depth - 1)]
    down = [(at + 1, at) for at in range(depth - 1)]
    level = lax.axis_index("z")
    where = jnp.stack(
        [lax.axis_index("core"), level * PLANE, level % GLOBALS, lax.axis_index("y")]
    )

    tokens = queries.shape[0]
    kinds = jnp.stack(
        [
            jnp.swapaxes(array.reshape(tokens, HEADS, HEAD_DIM), 0, 1)
            for array in (key_vectors, value_vectors)
        ],
        axis=1,
    ).reshape(2 * HEADS, tokens, HEAD_DIM)
    own = lax.all_to_all(kinds, PLANE_AXES, 0, 0, tiled=True).reshape(PLANE, BLOCK, HEAD_DIM)

    rows = jnp.stack(
        [key_blocks]
        + [
            lax.ppermute(key_blocks, "y", [(at, (at + step) % breadth) for at in range(breadth)])
            for step in range(1, breadth)
        ]
    )
    above = lax.ppermute(key_blocks[-1, WSEL:], "z", down)
    own, rows, above = lax.optimization_barrier((own, rows, above))

    sent = jnp.transpose(
        queries.reshape(2, BLOCK, HEADS, HEAD_DIM), (2, 0, 1, 3)
    ).reshape(2 * HEADS, BLOCK, HEAD_DIM)
    query = lax.all_to_all(sent, PLANE_AXES, 0, 0, tiled=True)

    def within(step):
        return [(at, at - at % GLOBALS + (at + step) % GLOBALS) for at in range(depth)]

    def across(step):
        return [(at, (at + GLOBALS * step) % depth) for at in range(depth)]

    other = swapped(own)
    parts = pick_globals(where, rows, above, own)
    held = added(
        parts[0], *[lax.ppermute(parts[step], "z", within(step)) for step in range(1, GLOBALS)]
    )
    halo_own = lax.ppermute(own[PLANE - WIN :], "z", up)
    halo_other = swapped(halo_own)

    half = PLANE // 4
    arrived = [lax.ppermute(held, "z", across(step)) for step in range(1, depth // GLOBALS)]
    after, _ = lax.optimization_barrier((query, held))
    far = attend_window(half, half, CHUNK, PLANE, where, rows, after, own, other)
    far, held, arrived = lax.optimization_barrier((far, held, arrived))
    held = added(held, *arrived)
    arrived = [lax.ppermute(held, "z", within(step)) for step in range(1, GLOBALS)]
    after, _ = lax.optimization_barrier((query, held))
    near = attend_window(0, half, 0, 2 * half, where, rows, after, own, other, halo_own, halo_other)
    near, held, arrived = lax.optimization_barrier((near, held, arrived))
    global_own = jnp.stack([held] + list(arrived))
    global_other = swapped(global_own)
    context = attend_global(where, rows, query, global_own, global_other, near, far)
    back = lax.all_to_all(context, PLANE_AXES, 0, 0, tiled=True)
    return jnp.transpose(
        back.reshape(HEADS, 2, BLOCK, HEAD_DIM), (1, 2, 0, 3)
    ).reshape(tokens, HEADS * HEAD_DIM)


def solution(mesh):
    fine = Mesh(mesh.devices.reshape(-1, 4, 4, 2), ("z",) + PLANE_AXES)
    tokens = P(("z",) + PLANE_AXES, None)
    return jax.shard_map(
        shards,
        mesh=fine,
        in_specs=(tokens, tokens, tokens, P(("z", "y"), None)),
        out_specs=tokens,
        check_vma=False,
    )
```

```python
import functools
import math

import jax
import jax.numpy as jnp
from jax import lax
from jax.experimental import pallas as pl
from jax.experimental.pallas import tpu as pltpu
from jax.sharding import Mesh
from jax.sharding import PartitionSpec as P

HEAD_DIM = 128
BLOCK = 128
WIN = 16
WSEL = 10
GLOBALS = 4
SLOTS = WSEL + GLOBALS
HEADS = 16
PLANE = 64
FACTOR = math.log2(math.e) / math.sqrt(HEAD_DIM)
UNROLL = 4
PLANE_AXES = ("y", "x", "core")


def row_of(where, row):
    return (where[2] + 4 - row // WIN) % 4, row % WIN


def pick_kernel(where, rows, above, kinds, out, buffer, sems):
    group, last = row_of(where, PLANE - 1)
    copies, present = [], []
    for slot in range(GLOBALS):
        place = jnp.maximum(rows[group, last, WSEL + slot], above[slot]) - where[1]
        held = (place >= 0) & (place < PLANE)
        source = kinds.at[jnp.where(held, place, 0)]
        copies.append(pltpu.make_async_copy(source, buffer.at[slot], sems.at[slot]))
        present.append(held)
    for copy in copies:
        copy.start()
    for slot in range(GLOBALS):
        copies[slot].wait()
        block = buffer[slot].astype(jnp.float32)
        out[slot] = jnp.where(present[slot], block, jnp.zeros_like(block))


def pick_globals(where, rows, above, kinds):
    scalars = pl.BlockSpec(memory_space=pltpu.SMEM)
    return pl.pallas_call(
        pick_kernel,
        out_shape=jax.ShapeDtypeStruct((GLOBALS, BLOCK, HEAD_DIM), jnp.float32),
        in_specs=[scalars, scalars, scalars, pl.BlockSpec(memory_space=pl.ANY)],
        out_specs=pl.BlockSpec(memory_space=pltpu.VMEM),
        scratch_shapes=[
            pltpu.VMEM((GLOBALS, BLOCK, HEAD_DIM), jnp.bfloat16),
            pltpu.SemaphoreType.DMA((GLOBALS,)),
        ],
        compiler_params=pltpu.CompilerParams(vmem_limit_bytes=20 << 20),
        name="pick_globals",
    )(where, rows, above, kinds)


def attend_kernel(
    where, rows, query, own, other, halo_own, halo_other, global_own, global_other,
    out, keys, values, scores, weights, sems,
):
    core = where[0]
    first = where[1]

    def fill(own_to, other_to):
        copies = [
            (own, own_to.at[pl.ds(0, PLANE)]),
            (other, other_to.at[pl.ds(0, PLANE)]),
            (halo_own, own_to.at[pl.ds(PLANE, WIN)]),
            (halo_other, other_to.at[pl.ds(PLANE, WIN)]),
            (global_own, own_to.at[pl.ds(PLANE + WIN, GLOBALS)]),
            (global_other, other_to.at[pl.ds(PLANE + WIN, GLOBALS)]),
        ]
        started = [
            pltpu.make_async_copy(source, target, sems.at[at])
            for at, (source, target) in enumerate(copies)
        ]
        for copy in started:
            copy.start()
        for copy in started:
            copy.wait()

    @pl.when(core == 0)
    def _():
        fill(keys, values)

    @pl.when(core != 0)
    def _():
        fill(values, keys)

    causal = lax.broadcasted_iota(jnp.int32, (BLOCK, BLOCK), 0) >= lax.broadcasted_iota(
        jnp.int32, (BLOCK, BLOCK), 1
    )

    def attend_block(at, lane):
        group, row = row_of(where, 2 * at + core)
        block_query = query[at]
        places, listed = [], []
        for slot in range(SLOTS):
            block_id = rows[group, row, slot]
            if slot < WSEL:
                offset = block_id - first
                place = jnp.where(offset >= 0, offset, offset + PLANE + WIN)
            else:
                place = PLANE + WIN + slot - WSEL
            listed.append(block_id >= 0)
            places.append(jnp.where(block_id >= 0, place, 0))
        highest = None
        for slot in range(0, SLOTS, 2):
            pair = jnp.concatenate([keys[places[slot]], keys[places[slot + 1]]], axis=0)
            both = lax.dot_general(
                block_query, pair, (((1,), (1,)), ((), ())), preferred_element_type=jnp.float32
            )
            for part in range(2):
                score = both[:, part * BLOCK : (part + 1) * BLOCK]
                allowed = causal if slot + part == 0 else listed[slot + part]
                score = jnp.where(allowed, score, -1e30)
                scores[lane, slot + part] = score
                highest = score if highest is None else jnp.maximum(highest, score)
        row_max = jnp.max(highest, axis=1, keepdims=True) * FACTOR
        row_max = jnp.broadcast_to(row_max, (BLOCK, BLOCK))
        total = None
        for slot in range(SLOTS):
            weight = jnp.exp2(scores[lane, slot] * FACTOR - row_max)
            total = weight if total is None else total + weight
            weights[lane, :, slot * BLOCK : (slot + 1) * BLOCK] = weight.astype(jnp.bfloat16)
        mixed = None
        for slot in range(0, SLOTS, 2):
            pair = jnp.concatenate([values[places[slot]], values[places[slot + 1]]], axis=0)
            term = jnp.dot(
                weights[lane, :, slot * BLOCK : (slot + 2) * BLOCK],
                pair,
                preferred_element_type=jnp.float32,
            )
            mixed = term if mixed is None else mixed + term
        denom = jnp.sum(total, axis=1, keepdims=True)
        out[at] = (mixed / denom).astype(jnp.bfloat16)

    def step(at, carry):
        for lane in range(UNROLL):
            attend_block(at * UNROLL + lane, lane)
        return carry

    lax.fori_loop(0, query.shape[0] // UNROLL, step, 0)


def attend(where, rows, query, own, other, halo_own, halo_other, global_own, global_other):
    scalars = pl.BlockSpec(memory_space=pltpu.SMEM)
    whole = pl.BlockSpec(memory_space=pltpu.VMEM)
    left = pl.BlockSpec(memory_space=pl.ANY)
    span = PLANE + WIN + GLOBALS
    pairs = query.shape[0] * SLOTS * BLOCK * BLOCK
    return pl.pallas_call(
        attend_kernel,
        out_shape=jax.ShapeDtypeStruct(query.shape, jnp.bfloat16),
        in_specs=[scalars, scalars, whole] + [left] * 6,
        out_specs=whole,
        scratch_shapes=[
            pltpu.VMEM((span, BLOCK, HEAD_DIM), jnp.bfloat16),
            pltpu.VMEM((span, BLOCK, HEAD_DIM), jnp.bfloat16),
            pltpu.VMEM((UNROLL, SLOTS, BLOCK, BLOCK), jnp.float32),
            pltpu.VMEM((UNROLL, BLOCK, SLOTS * BLOCK), jnp.bfloat16),
            pltpu.SemaphoreType.DMA((6,)),
        ],
        compiler_params=pltpu.CompilerParams(vmem_limit_bytes=24 << 20),
        cost_estimate=pl.CostEstimate(
            flops=4 * pairs * HEAD_DIM, bytes_accessed=8 << 20, transcendentals=pairs
        ),
        name="attend",
    )(where, rows, query, own, other, halo_own, halo_other, global_own, global_other)


def swapped(value):
    return lax.ppermute(value, "core", [(0, 1), (1, 0)])


def shards(queries, key_vectors, value_vectors, key_blocks):
    depth = lax.axis_size("z")
    breadth = lax.axis_size("y")
    up = [(at, at + 1) for at in range(depth - 1)]
    down = [(at + 1, at) for at in range(depth - 1)]
    where = jnp.stack(
        [lax.axis_index("core"), lax.axis_index("z") * PLANE, lax.axis_index("y")]
    )

    tokens = queries.shape[0]
    kinds = jnp.stack(
        [
            jnp.swapaxes(array.reshape(tokens, HEADS, HEAD_DIM), 0, 1)
            for array in (key_vectors, value_vectors)
        ],
        axis=1,
    ).reshape(2 * HEADS, tokens, HEAD_DIM)
    own = lax.all_to_all(kinds, PLANE_AXES, 0, 0, tiled=True).reshape(PLANE, BLOCK, HEAD_DIM)

    rows = jnp.stack(
        [key_blocks]
        + [
            lax.ppermute(key_blocks, "y", [(at, (at + step) % breadth) for at in range(breadth)])
            for step in range(1, breadth)
        ]
    )
    above = lax.ppermute(key_blocks[-1, WSEL:], "z", down)
    own, rows, above = lax.optimization_barrier((own, rows, above))

    query = lax.all_to_all(
        jnp.transpose(
            queries.reshape(2, BLOCK, HEADS, HEAD_DIM), (2, 0, 1, 3)
        ).reshape(2 * HEADS, BLOCK, HEAD_DIM),
        PLANE_AXES, 0, 0, tiled=True,
    )

    other = swapped(own)
    halo_own = lax.ppermute(own[PLANE - WIN :], "z", up)

    part = pick_globals(where, rows, above, own)
    global_own = lax.psum(part, "z").astype(jnp.bfloat16)
    halo_own, global_own = lax.optimization_barrier((halo_own, global_own))
    global_other = swapped(global_own)
    halo_other = swapped(halo_own)

    context = attend(
        where, rows, query, own, other, halo_own, halo_other, global_own, global_other
    )
    back = lax.all_to_all(context, PLANE_AXES, 0, 0, tiled=True)
    return jnp.transpose(
        back.reshape(HEADS, 2, BLOCK, HEAD_DIM), (1, 2, 0, 3)
    ).reshape(tokens, HEADS * HEAD_DIM)


def solution(mesh):
    fine = Mesh(mesh.devices.reshape(-1, 4, 4, 2), ("z",) + PLANE_AXES)
    tokens = P(("z",) + PLANE_AXES, None)
    return jax.shard_map(
        shards,
        mesh=fine,
        in_specs=(tokens, tokens, tokens, P(("z", "y"), None)),
        out_specs=tokens,
        check_vma=False,
    )
```

```python
import functools
import math

import jax
import jax.numpy as jnp
from jax import lax
from jax.experimental import pallas as pl
from jax.experimental.pallas import tpu as pltpu
from jax.sharding import Mesh
from jax.sharding import PartitionSpec as P

HEAD_DIM = 128
BLOCK = 128
WIN = 16
WSEL = 10
GLOBALS = 4
SLOTS = WSEL + GLOBALS
HEADS = 16
PLANE = 64
CHUNK = 16
FACTOR = math.log2(math.e) / math.sqrt(HEAD_DIM)
UNROLL = 4
MERGED = 8
PLANE_AXES = ("y", "x", "core")

SCALARS = pl.BlockSpec(memory_space=pltpu.SMEM)
WHOLE = pl.BlockSpec(memory_space=pltpu.VMEM)
LEFT = pl.BlockSpec(memory_space=pl.ANY)


def pack_kernel(queries, keys, values, out, query_buf, key_buf, value_buf, arrived, sems):
    def moves():
        for head in range(HEADS):
            columns = pl.ds(head * HEAD_DIM, HEAD_DIM)
            yield 0, key_buf.at[:, :, columns], out.at[2 * head, pl.ds(0, 2)]
            yield 1, value_buf.at[:, :, columns], out.at[2 * head + 1, pl.ds(0, 2)]
            yield 2, query_buf.at[0, :, columns], out.at[2 * head, 2]
            yield 2, query_buf.at[1, :, columns], out.at[2 * head + 1, 2]

    loads = [
        pltpu.make_async_copy(source, target, arrived.at[at])
        for at, (source, target) in enumerate(
            [(keys, key_buf), (values, value_buf), (queries, query_buf)]
        )
    ]
    stores = [
        (array, pltpu.make_async_copy(source, target, sems.at[at]))
        for at, (array, source, target) in enumerate(moves())
    ]
    for load in loads:
        load.start()
    for at, load in enumerate(loads):
        load.wait()
        for array, store in stores:
            if array == at:
                store.start()
    for _, store in stores:
        store.wait()


def pack(*arrays):
    arrays = [array.reshape(2, BLOCK, HEADS * HEAD_DIM) for array in arrays]
    return pl.pallas_call(
        pack_kernel,
        out_shape=jax.ShapeDtypeStruct((2 * HEADS, 3, BLOCK, HEAD_DIM), jnp.bfloat16),
        in_specs=[LEFT] * 3,
        out_specs=LEFT,
        scratch_shapes=[pltpu.VMEM(array.shape, array.dtype) for array in arrays]
        + [pltpu.SemaphoreType.DMA((3,)), pltpu.SemaphoreType.DMA((4 * HEADS,))],
        compiler_params=pltpu.CompilerParams(vmem_limit_bytes=56 << 20),
        name="pack",
    )(*arrays)


def pick_kernel(where, rows, above, kinds, out, buffer, sems):
    group, last = row_of(where, PLANE // 2 - 1, 1)
    copies, present = [], []
    for slot in range(GLOBALS):
        place = jnp.maximum(rows[group, last, WSEL + slot], above[slot]) - where[1]
        held = (place >= 0) & (place < PLANE)
        place = jnp.where(held, place, 0)
        source = kinds.at[place // 2, place % 2]
        copies.append(pltpu.make_async_copy(source, buffer.at[slot], sems.at[slot]))
        present.append(held)
    for copy in copies:
        copy.start()
    for slot in range(GLOBALS):
        copies[slot].wait()
        block = buffer[slot]
        out[slot] = jnp.where(present[slot], block, jnp.zeros_like(block))


def pick_globals(where, rows, above, kinds):
    return pl.pallas_call(
        pick_kernel,
        out_shape=jax.ShapeDtypeStruct((GLOBALS, BLOCK, HEAD_DIM), jnp.bfloat16),
        in_specs=[SCALARS, SCALARS, SCALARS, LEFT],
        out_specs=WHOLE,
        scratch_shapes=[
            pltpu.VMEM((GLOBALS, BLOCK, HEAD_DIM), jnp.bfloat16),
            pltpu.SemaphoreType.DMA((GLOBALS,)),
        ],
        compiler_params=pltpu.CompilerParams(vmem_limit_bytes=12 << 20),
        name="pick_globals",
    )(where, rows, above, kinds)


def row_of(where, at, core):
    row = 2 * at + core
    return (where[2] + 4 - row // CHUNK) % 4, row % CHUNK


def two_blocks(blocks, one, two):
    return jnp.concatenate([blocks[one // 2, one % 2], blocks[two // 2, two % 2]], axis=0)


def window_kernel(start, low, high, with_halo, where, rows, own, other, *refs):
    if with_halo:
        halo_own, halo_other, *refs = refs
    out, out_stats, keys, values, scores, weights, sems = refs
    core, first = where[0], where[1]
    count = out.shape[0]
    chunks = (high - low) // CHUNK

    def copies(own_to, other_to, at):
        if at < chunks:
            source = pl.ds((low + at * CHUNK) // 2, CHUNK // 2)
            target = pl.ds(at * CHUNK // 2, CHUNK // 2)
            for kind, (array, to) in enumerate([(own, own_to), (other, other_to)]):
                yield pltpu.make_async_copy(
                    array.at[source, pl.ds(0, 2)], to.at[target], sems.at[kind, at]
                )
        else:
            target = pl.ds(at * CHUNK // 2, WIN // 2)
            yield pltpu.make_async_copy(halo_own, own_to.at[target], sems.at[0, at])
            yield pltpu.make_async_copy(halo_other, other_to.at[target], sems.at[1, at])

    parts = list(range(chunks)) + ([chunks] if with_halo else [])

    @pl.when(core == 0)
    def _():
        for part in parts:
            for copy in copies(keys, values, part):
                copy.start()

    @pl.when(core != 0)
    def _():
        for part in parts:
            for copy in copies(values, keys, part):
                copy.start()

    needed = {}
    for part in parts:
        step = 0
        if part < chunks:
            step = max(0, (low + part * CHUNK - 2 * start) // (2 * UNROLL))
        needed.setdefault(step, []).append(part)

    causal = lax.broadcasted_iota(jnp.int32, (BLOCK, BLOCK), 0) >= lax.broadcasted_iota(
        jnp.int32, (BLOCK, BLOCK), 1
    )

    left = lax.broadcasted_iota(jnp.int32, (BLOCK, BLOCK), 1) < BLOCK // 2

    def attend_block(at, lane):
        group, row = row_of(where, start + at, core)
        block_query = own[start + at, 2]
        places, listed = [], []
        for slot in range(WSEL):
            block_id = rows[group, row, slot]
            place = block_id - first - low
            if with_halo:
                place = jnp.where(place >= 0, place, place + high + WIN)
            listed.append(block_id >= 0)
            places.append(jnp.where(block_id >= 0, place, 0))
        highest = None
        for slot in range(0, WSEL, 2):
            pair = two_blocks(keys, places[slot], places[slot + 1])
            both = lax.dot_general(
                block_query, pair, (((1,), (1,)), ((), ())), preferred_element_type=jnp.float32
            )
            for part in range(2):
                score = both[:, part * BLOCK : (part + 1) * BLOCK]
                if slot + part == 0:
                    score = jnp.where(causal, score, -1e30)
                elif with_halo:
                    score = jnp.where(listed[slot + part], score, -1e30)
                scores[lane, slot + part] = score
                highest = score if highest is None else jnp.maximum(highest, score)
        row_max = jnp.max(highest, axis=1, keepdims=True) * FACTOR
        row_max = jnp.broadcast_to(row_max, (BLOCK, BLOCK))
        total = None
        for slot in range(WSEL):
            weight = jnp.exp2(scores[lane, slot] * FACTOR - row_max)
            total = weight if total is None else total + weight
            weights[lane, :, slot * BLOCK : (slot + 1) * BLOCK] = weight.astype(jnp.bfloat16)
        row_sum = jnp.broadcast_to(jnp.sum(total, axis=1, keepdims=True), (BLOCK, BLOCK))
        out_stats[at] = jnp.where(left, row_max, row_sum)
        mixed = None
        for slot in range(0, WSEL, 2):
            pair = two_blocks(values, places[slot], places[slot + 1])
            term = jnp.dot(
                weights[lane, :, slot * BLOCK : (slot + 2) * BLOCK],
                pair,
                preferred_element_type=jnp.float32,
            )
            mixed = term if mixed is None else mixed + term
        out[at] = mixed

    def step(at, carry):
        for when, needs in needed.items():

            @pl.when(at == when)
            def _(needs=needs):
                for part in needs:
                    for copy in copies(keys, values, part):
                        copy.wait()

        for lane in range(UNROLL):
            attend_block(at * UNROLL + lane, lane)
        return carry

    lax.fori_loop(0, count // UNROLL, step, 0)


def attend_window(start, count, low, high, where, rows, own, other, *halo):
    span = high - low + (WIN if halo else 0)
    sums = jax.ShapeDtypeStruct((count, BLOCK, HEAD_DIM), jnp.float32)
    pairs = count * WSEL * BLOCK * BLOCK
    return pl.pallas_call(
        functools.partial(window_kernel, start, low, high, bool(halo)),
        out_shape=[sums] * 2,
        in_specs=[SCALARS, SCALARS, WHOLE] + [LEFT] * (1 + len(halo)),
        out_specs=[WHOLE] * 2,
        scratch_shapes=[
            pltpu.VMEM((span // 2, 2, BLOCK, HEAD_DIM), jnp.bfloat16),
            pltpu.VMEM((span // 2, 2, BLOCK, HEAD_DIM), jnp.bfloat16),
            pltpu.VMEM((UNROLL, WSEL, BLOCK, BLOCK), jnp.float32),
            pltpu.VMEM((UNROLL, BLOCK, WSEL * BLOCK), jnp.bfloat16),
            pltpu.SemaphoreType.DMA((2, span // CHUNK)),
        ],
        compiler_params=pltpu.CompilerParams(vmem_limit_bytes=12 << 20),
        cost_estimate=pl.CostEstimate(
            flops=4 * pairs * HEAD_DIM, bytes_accessed=8 << 20, transcendentals=pairs
        ),
        name="attend_near" if halo else "attend_far",
    )(where, rows, own, other, *halo)


def global_kernel(
    where, rows, own, other, query, near_sum, near_stats, far_sum, far_stats,
    out, keys, values, weights, sems,
):
    core, at = where[0], pl.program_id(0)

    @pl.when(at == 0)
    def _():
        def fill(own_to, other_to):
            copies = [
                pltpu.make_async_copy(own, own_to, sems.at[0]),
                pltpu.make_async_copy(other, other_to, sems.at[1]),
            ]
            for copy in copies:
                copy.start()
            for copy in copies:
                copy.wait()

        @pl.when(core == 0)
        def _():
            fill(keys, values)

        @pl.when(core != 0)
        def _():
            fill(values, keys)

    def merge(lane, sums, stats):
        group, row = row_of(where, at * MERGED + lane, core)
        block_query = query[lane, 0]
        held, highest = [], None
        for slot in range(0, GLOBALS, 2):
            pair = jnp.concatenate([keys[slot], keys[slot + 1]], axis=0)
            both = lax.dot_general(
                block_query, pair, (((1,), (1,)), ((), ())), preferred_element_type=jnp.float32
            )
            for part in range(2):
                score = both[:, part * BLOCK : (part + 1) * BLOCK]
                listed = rows[group, row, WSEL + slot + part] >= 0
                score = jnp.where(listed, score, -1e30)
                held.append(score)
                highest = score if highest is None else jnp.maximum(highest, score)
        window_max = stats[lane, :, :1]
        row_max = jnp.maximum(jnp.max(highest, axis=1, keepdims=True) * FACTOR, window_max)
        shrink = jnp.exp2(window_max - row_max)
        row_max = jnp.broadcast_to(row_max, (BLOCK, BLOCK))
        total = None
        for slot in range(GLOBALS):
            weight = jnp.exp2(held[slot] * FACTOR - row_max)
            total = weight if total is None else total + weight
            weights[lane, :, slot * BLOCK : (slot + 1) * BLOCK] = weight.astype(jnp.bfloat16)
        mixed = sums[lane] * shrink
        for slot in range(0, GLOBALS, 2):
            pair = jnp.concatenate([values[slot], values[slot + 1]], axis=0)
            mixed = mixed + jnp.dot(
                weights[lane, :, slot * BLOCK : (slot + 2) * BLOCK],
                pair,
                preferred_element_type=jnp.float32,
            )
        window_sum = stats[lane, :, BLOCK // 2 : BLOCK // 2 + 1]
        denom = jnp.sum(total, axis=1, keepdims=True) + window_sum * shrink
        out[lane] = (mixed / denom).astype(jnp.bfloat16)

    @pl.when(at < pl.num_programs(0) // 2)
    def _():
        for lane in range(MERGED):
            merge(lane, near_sum, near_stats)

    @pl.when(at >= pl.num_programs(0) // 2)
    def _():
        for lane in range(MERGED):
            merge(lane, far_sum, far_stats)


def attend_global(where, rows, received, own, other, near, far):
    count = received.shape[0]
    steps = count // MERGED
    pairs = count * GLOBALS * BLOCK * BLOCK
    tile = (MERGED, BLOCK, HEAD_DIM)
    of_near = pl.BlockSpec(tile, lambda at: (jnp.minimum(at, steps // 2 - 1), 0, 0))
    of_far = pl.BlockSpec(tile, lambda at: (jnp.maximum(at - steps // 2, 0), 0, 0))
    return pl.pallas_call(
        global_kernel,
        grid=(steps,),
        out_shape=jax.ShapeDtypeStruct((count, BLOCK, HEAD_DIM), jnp.bfloat16),
        in_specs=[SCALARS, SCALARS, LEFT, LEFT]
        + [pl.BlockSpec((MERGED, 1, BLOCK, HEAD_DIM), lambda at: (at, 2, 0, 0))]
        + [of_near, of_near, of_far, of_far],
        out_specs=pl.BlockSpec(tile, lambda at: (at, 0, 0)),
        scratch_shapes=[
            pltpu.VMEM((GLOBALS, BLOCK, HEAD_DIM), jnp.bfloat16),
            pltpu.VMEM((GLOBALS, BLOCK, HEAD_DIM), jnp.bfloat16),
            pltpu.VMEM((MERGED, BLOCK, GLOBALS * BLOCK), jnp.bfloat16),
            pltpu.SemaphoreType.DMA((2,)),
        ],
        compiler_params=pltpu.CompilerParams(vmem_limit_bytes=57 << 20),
        cost_estimate=pl.CostEstimate(
            flops=4 * pairs * HEAD_DIM, bytes_accessed=8 << 20, transcendentals=pairs
        ),
        name="attend_global",
    )(where, rows, own, other, received, *near, *far)


def swapped(value):
    return lax.ppermute(value, "core", [(0, 1), (1, 0)])


def shards(queries, key_vectors, value_vectors, key_blocks):
    depth = lax.axis_size("z")
    breadth = lax.axis_size("y")
    up = [(at, at + 1) for at in range(depth - 1)]
    down = [(at + 1, at) for at in range(depth - 1)]
    where = jnp.stack(
        [lax.axis_index("core"), lax.axis_index("z") * PLANE, lax.axis_index("y")]
    )

    received = lax.all_to_all(
        pack(queries, key_vectors, value_vectors), PLANE_AXES, 0, 0, tiled=True
    )

    rows = jnp.stack(
        [key_blocks]
        + [
            lax.ppermute(key_blocks, "y", [(at, (at + step) % breadth) for at in range(breadth)])
            for step in range(1, breadth)
        ]
    )
    above = lax.ppermute(key_blocks[-1, WSEL:], "z", down)
    own, rows, above = lax.optimization_barrier((received, rows, above))
    other = swapped(own)
    halo_own = lax.ppermute(own[-WIN // 2 :, :2], "z", up)

    half = PLANE // 4
    part = pick_globals(where, rows, above, own).reshape(depth, -1, HEAD_DIM)
    after, _ = lax.optimization_barrier((own, part))
    pieces = lax.all_to_all(part, "z", 0, 0, tiled=True)
    far = attend_window(half, half, CHUNK, PLANE, where, rows, after, other)
    far, pieces, halo_own = lax.optimization_barrier((far, pieces, halo_own))
    halo_other = swapped(halo_own)
    summed = jnp.sum(pieces.astype(jnp.float32), axis=0, keepdims=True).astype(jnp.bfloat16)
    spread = jnp.broadcast_to(summed, part.shape)
    after, _ = lax.optimization_barrier((own, spread))
    gathered = lax.all_to_all(spread, "z", 0, 0, tiled=True)
    near = attend_window(0, half, 0, 2 * half, where, rows, after, other, halo_own, halo_other)
    near, gathered = lax.optimization_barrier((near, gathered))
    global_own = gathered.reshape(GLOBALS, BLOCK, HEAD_DIM)
    global_other = swapped(global_own)
    context = attend_global(where, rows, own, global_own, global_other, near, far)
    back = lax.all_to_all(context, PLANE_AXES, 0, 0, tiled=True)
    return jnp.transpose(
        back.reshape(HEADS, 2, BLOCK, HEAD_DIM), (1, 2, 0, 3)
    ).reshape(queries.shape)


def solution(mesh):
    fine = Mesh(mesh.devices.reshape(-1, 4, 4, 2), ("z",) + PLANE_AXES)
    tokens = P(("z",) + PLANE_AXES, None)
    return jax.shard_map(
        shards,
        mesh=fine,
        in_specs=(tokens, tokens, tokens, P(("z", "y"), None)),
        out_specs=tokens,
        check_vma=False,
    )
```

```python
import functools
import math

import jax
import jax.numpy as jnp
from jax import lax
from jax.experimental import pallas as pl
from jax.experimental.pallas import tpu as pltpu
from jax.sharding import Mesh
from jax.sharding import PartitionSpec as P

HEAD_DIM = 128
BLOCK = 128
WIN = 16
WSEL = 10
GLOBALS = 4
SLOTS = WSEL + GLOBALS
HEADS = 16
PLANE = 64
CHUNK = 16
FACTOR = math.log2(math.e) / math.sqrt(HEAD_DIM)
UNROLL = 4
PLANE_AXES = ("y", "x", "core")
Z_AXES = ("far", "near")

SCALARS = pl.BlockSpec(memory_space=pltpu.SMEM)
WHOLE = pl.BlockSpec(memory_space=pltpu.VMEM)
LEFT = pl.BlockSpec(memory_space=pl.ANY)


def pack_kernel(queries, keys, values, out, query_buf, key_buf, value_buf, arrived, sems):
    def moves():
        for head in range(HEADS):
            columns = pl.ds(head * HEAD_DIM, HEAD_DIM)
            yield 0, key_buf.at[:, :, columns], out.at[2 * head, pl.ds(0, 2)]
            yield 1, value_buf.at[:, :, columns], out.at[2 * head + 1, pl.ds(0, 2)]
            yield 2, query_buf.at[0, :, columns], out.at[2 * head, 2]
            yield 2, query_buf.at[1, :, columns], out.at[2 * head + 1, 2]

    loads = [
        pltpu.make_async_copy(source, target, arrived.at[at])
        for at, (source, target) in enumerate(
            [(keys, key_buf), (values, value_buf), (queries, query_buf)]
        )
    ]
    stores = [
        (array, pltpu.make_async_copy(source, target, sems.at[at]))
        for at, (array, source, target) in enumerate(moves())
    ]
    for load in loads:
        load.start()
    for at, load in enumerate(loads):
        load.wait()
        for array, store in stores:
            if array == at:
                store.start()
    for _, store in stores:
        store.wait()


def pack(*arrays):
    arrays = [array.reshape(2, BLOCK, HEADS * HEAD_DIM) for array in arrays]
    return pl.pallas_call(
        pack_kernel,
        out_shape=jax.ShapeDtypeStruct((2 * HEADS, 3, BLOCK, HEAD_DIM), jnp.bfloat16),
        in_specs=[LEFT] * 3,
        out_specs=LEFT,
        scratch_shapes=[pltpu.VMEM(array.shape, array.dtype) for array in arrays]
        + [pltpu.SemaphoreType.DMA((3,)), pltpu.SemaphoreType.DMA((4 * HEADS,))],
        compiler_params=pltpu.CompilerParams(vmem_limit_bytes=56 << 20),
        name="pack",
    )(*arrays)


def pick_kernel(where, rows, above, kinds, out, buffer, sems):
    group, last = row_of(where, PLANE // 2 - 1, 1)
    copies, present = [], []
    for slot in range(GLOBALS):
        place = jnp.maximum(rows[group, last, WSEL + slot], above[slot]) - where[1]
        held = (place >= 0) & (place < PLANE)
        place = jnp.where(held, place, 0)
        source = kinds.at[place // 2, place % 2]
        copies.append(pltpu.make_async_copy(source, buffer.at[slot], sems.at[slot]))
        present.append(held)
    for copy in copies:
        copy.start()
    for slot in range(GLOBALS):
        copies[slot].wait()
        block = buffer[slot]
        out[slot] = jnp.where(present[slot], block, jnp.zeros_like(block))


def pick_globals(where, rows, above, kinds):
    return pl.pallas_call(
        pick_kernel,
        out_shape=jax.ShapeDtypeStruct((GLOBALS, BLOCK, HEAD_DIM), jnp.bfloat16),
        in_specs=[SCALARS, SCALARS, SCALARS, LEFT],
        out_specs=WHOLE,
        scratch_shapes=[
            pltpu.VMEM((GLOBALS, BLOCK, HEAD_DIM), jnp.bfloat16),
            pltpu.SemaphoreType.DMA((GLOBALS,)),
        ],
        compiler_params=pltpu.CompilerParams(vmem_limit_bytes=12 << 20),
        name="pick_globals",
    )(where, rows, above, kinds)


def row_of(where, at, core):
    row = 2 * at + core
    return (where[2] + 4 - row // CHUNK) % 4, row % CHUNK


def two_blocks(blocks, one, two):
    return jnp.concatenate([blocks[one // 2, one % 2], blocks[two // 2, two % 2]], axis=0)


def attend_kernel(start, high, kept, where, rows, own, other, global_own, global_other, *refs):
    if kept:
        halo_own, halo_other, before, *refs = refs
    out, keys, values, scores, weights, sems = refs
    core, first = where[0], where[1]
    chunks = high // CHUNK
    halo_at = high
    global_at = high + (WIN if kept else 0)
    count = kept if kept else out.shape[0]

    def copies(own_to, other_to, at):
        if at < chunks:
            source = pl.ds(at * CHUNK // 2, CHUNK // 2)
            pairs = [(own.at[source, pl.ds(0, 2)], own_to), (other.at[source, pl.ds(0, 2)], other_to)]
            target = source
        elif at == chunks:
            pairs = [(global_own, own_to), (global_other, other_to)]
            target = pl.ds(global_at // 2, GLOBALS // 2)
        else:
            pairs = [(halo_own, own_to), (halo_other, other_to)]
            target = pl.ds(halo_at // 2, WIN // 2)
        for kind, (array, to) in enumerate(pairs):
            yield pltpu.make_async_copy(array, to.at[target], sems.at[kind, at])

    parts = list(range(chunks + (2 if kept else 1)))

    @pl.when(core == 0)
    def _():
        for part in parts:
            for copy in copies(keys, values, part):
                copy.start()

    @pl.when(core != 0)
    def _():
        for part in parts:
            for copy in copies(values, keys, part):
                copy.start()

    if kept:
        out[kept:] = before[...]

    needed = {}
    for part in parts:
        step = 0
        if part < chunks:
            step = max(0, (part * CHUNK - 2 * start) // (2 * UNROLL))
        needed.setdefault(step, []).append(part)

    causal = lax.broadcasted_iota(jnp.int32, (BLOCK, BLOCK), 0) >= lax.broadcasted_iota(
        jnp.int32, (BLOCK, BLOCK), 1
    )

    def place_of(at, slot):
        group, row = row_of(where, start + at, core)
        block_id = rows[group, row, slot]
        if slot < WSEL:
            place = block_id - first
            if kept:
                place = jnp.where(place >= 0, place, place + halo_at + WIN)
        else:
            place = global_at + slot - WSEL
        return jnp.where(block_id >= 0, place, 0), block_id >= 0

    def score_phase(at, lane):
        block_query = own[start + at, 2]
        highest = None
        for slot in range(0, SLOTS, 2):
            one, listed_one = place_of(at, slot)
            two, listed_two = place_of(at, slot + 1)
            both = lax.dot_general(
                block_query, two_blocks(keys, one, two), (((1,), (1,)), ((), ())),
                preferred_element_type=jnp.float32,
            )
            for part, listed in enumerate([listed_one, listed_two]):
                score = both[:, part * BLOCK : (part + 1) * BLOCK]
                if slot + part == 0:
                    score = jnp.where(causal, score, -1e30)
                elif kept or slot + part >= WSEL:
                    score = jnp.where(listed, score, -1e30)
                scores[lane, slot + part] = score
                highest = score if highest is None else jnp.maximum(highest, score)
        row_max = jnp.max(highest, axis=1, keepdims=True) * FACTOR
        return jnp.broadcast_to(row_max, (BLOCK, BLOCK))

    def weight_phase(lane, row_max):
        total = None
        for slot in range(SLOTS):
            weight = jnp.exp2(scores[lane, slot] * FACTOR - row_max)
            total = weight if total is None else total + weight
            weights[lane, :, slot * BLOCK : (slot + 1) * BLOCK] = weight.astype(jnp.bfloat16)
        return jnp.sum(total, axis=1, keepdims=True)

    def value_phase(at, lane, denom):
        mixed = None
        for slot in range(0, SLOTS, 2):
            one, two = place_of(at, slot)[0], place_of(at, slot + 1)[0]
            term = jnp.dot(
                weights[lane, :, slot * BLOCK : (slot + 2) * BLOCK],
                two_blocks(values, one, two),
                preferred_element_type=jnp.float32,
            )
            mixed = term if mixed is None else mixed + term
        out[at] = (mixed / denom).astype(jnp.bfloat16)

    def step(at, carry):
        for when, needs in needed.items():

            @pl.when(at == when)
            def _(needs=needs):
                for part in needs:
                    for copy in copies(keys, values, part):
                        copy.wait()

        at = at * UNROLL
        row_max, denom = score_phase(at, 0), None
        for lane in range(UNROLL):
            following = score_phase(at + lane + 1, lane + 1) if lane + 1 < UNROLL else None
            found = weight_phase(lane, row_max)
            if lane:
                value_phase(at + lane - 1, lane - 1, denom)
            row_max, denom = following, found
        value_phase(at + UNROLL - 1, UNROLL - 1, denom)
        return carry

    lax.fori_loop(0, count // UNROLL, step, 0)


def attend(start, high, where, rows, own, other, global_own, global_other, *halo):
    total = own.shape[0] - start
    kept = total - halo[-1].shape[0] if halo else 0
    count = kept if kept else total
    span = high + GLOBALS + (WIN if kept else 0)
    pairs = count * SLOTS * BLOCK * BLOCK
    return pl.pallas_call(
        functools.partial(attend_kernel, start, high, kept),
        out_shape=jax.ShapeDtypeStruct((total, BLOCK, HEAD_DIM), jnp.bfloat16),
        in_specs=[SCALARS, SCALARS, WHOLE]
        + [LEFT] * 3
        + ([LEFT, LEFT, WHOLE] if kept else []),
        out_specs=WHOLE,
        scratch_shapes=[
            pltpu.VMEM((span // 2, 2, BLOCK, HEAD_DIM), jnp.bfloat16),
            pltpu.VMEM((span // 2, 2, BLOCK, HEAD_DIM), jnp.bfloat16),
            pltpu.VMEM((UNROLL, SLOTS, BLOCK, BLOCK), jnp.float32),
            pltpu.VMEM((UNROLL, BLOCK, SLOTS * BLOCK), jnp.bfloat16),
            pltpu.SemaphoreType.DMA((2, high // CHUNK + 2)),
        ],
        compiler_params=pltpu.CompilerParams(vmem_limit_bytes=24 << 20),
        cost_estimate=pl.CostEstimate(
            flops=4 * pairs * HEAD_DIM, bytes_accessed=8 << 20, transcendentals=pairs
        ),
        name="attend_first" if kept else "attend_rest",
    )(where, rows, own, other, global_own, global_other, *halo)


def swapped(value):
    return lax.ppermute(value, "core", [(0, 1), (1, 0)])


def shards(queries, key_vectors, value_vectors, key_blocks):
    depth = lax.axis_size(Z_AXES)
    breadth = lax.axis_size("y")
    up = [(at, at + 1) for at in range(depth - 1)]
    down = [(at + 1, at) for at in range(depth - 1)]
    where = jnp.stack(
        [lax.axis_index("core"), lax.axis_index(Z_AXES) * PLANE, lax.axis_index("y")]
    )

    received = lax.all_to_all(
        pack(queries, key_vectors, value_vectors), PLANE_AXES, 0, 0, tiled=True
    )

    rows = jnp.stack(
        [key_blocks]
        + [
            lax.ppermute(key_blocks, "y", [(at, (at + step) % breadth) for at in range(breadth)])
            for step in range(1, breadth)
        ]
    )
    above = lax.ppermute(key_blocks[-1, WSEL:], Z_AXES, down)
    own, rows, above = lax.optimization_barrier((received, rows, above))
    other = swapped(own)

    def spread(value, axis):
        copies = jnp.broadcast_to(value[None], (GLOBALS,) + value.shape)
        return lax.all_to_all(copies, axis, 0, 0, tiled=True)

    def summed(values):
        return jnp.sum(values.astype(jnp.float32), axis=0).astype(jnp.bfloat16)

    part = pick_globals(where, rows, above, own)
    held = summed(lax.all_to_all(part, "near", 0, 0, tiled=True))
    held = summed(spread(held, "far"))
    global_own = spread(held, "near")
    last, global_own = lax.optimization_barrier((own[-WIN // 2 :, :2], global_own))
    pair = (GLOBALS // 2, 2, BLOCK, HEAD_DIM)
    global_own = global_own.reshape(pair)
    global_other = swapped(global_own)
    halo_own = lax.ppermute(last, Z_AXES, up)
    rest = attend(
        WIN // 2, PLANE, where, rows, own, other, global_own, global_other
    )
    rest, halo_own = lax.optimization_barrier((rest, halo_own))
    context = attend(
        0, CHUNK, where, rows, own, other, global_own, global_other,
        halo_own, swapped(halo_own), rest,
    )
    back = lax.all_to_all(context, PLANE_AXES, 0, 0, tiled=True)
    return jnp.transpose(
        back.reshape(HEADS, 2, BLOCK, HEAD_DIM), (1, 2, 0, 3)
    ).reshape(queries.shape)


def solution(mesh):
    fine = Mesh(mesh.devices.reshape(-1, GLOBALS, 4, 4, 2), Z_AXES + PLANE_AXES)
    tokens = P(Z_AXES + PLANE_AXES, None)
    return jax.shard_map(
        shards,
        mesh=fine,
        in_specs=(tokens, tokens, tokens, P(Z_AXES + ("y",), None)),
        out_specs=tokens,
        check_vma=False,
    )
```

```python
import functools
import math

import jax
import jax.numpy as jnp
from jax import lax
from jax.experimental import pallas as pl
from jax.experimental.pallas import tpu as pltpu
from jax.sharding import Mesh
from jax.sharding import PartitionSpec as P

HEAD_DIM = 128
BLOCK = 128
WIN = 16
WSEL = 10
GLOBALS = 4
SLOTS = WSEL + GLOBALS
HEADS = 16
PLANE = 64
CHUNK = 16
FACTOR = math.log2(math.e) / math.sqrt(HEAD_DIM)
UNROLL = 4
PLANE_AXES = ("y", "x", "core")

SCALARS = pl.BlockSpec(memory_space=pltpu.SMEM)
WHOLE = pl.BlockSpec(memory_space=pltpu.VMEM)
LEFT = pl.BlockSpec(memory_space=pl.ANY)


def pack_kernel(queries, keys, values, out, sent, query_buf, key_buf, value_buf, arrived, sems):
    def moves():
        for head in range(HEADS):
            columns = pl.ds(head * HEAD_DIM, HEAD_DIM)
            yield 0, key_buf.at[:, :, columns], out.at[2 * head]
            yield 1, value_buf.at[:, :, columns], out.at[2 * head + 1]
            yield 2, query_buf.at[0, :, columns], sent.at[2 * head]
            yield 2, query_buf.at[1, :, columns], sent.at[2 * head + 1]

    loads = [
        pltpu.make_async_copy(source, target, arrived.at[at])
        for at, (source, target) in enumerate(
            [(keys, key_buf), (values, value_buf), (queries, query_buf)]
        )
    ]
    stores = [
        (array, pltpu.make_async_copy(source, target, sems.at[at]))
        for at, (array, source, target) in enumerate(moves())
    ]
    for load in loads:
        load.start()
    for at, load in enumerate(loads):
        load.wait()
        for array, store in stores:
            if array == at:
                store.start()
    for _, store in stores:
        store.wait()


def pack(*arrays):
    arrays = [array.reshape(2, BLOCK, HEADS * HEAD_DIM) for array in arrays]
    return pl.pallas_call(
        pack_kernel,
        out_shape=[
            jax.ShapeDtypeStruct((2 * HEADS, 2, BLOCK, HEAD_DIM), jnp.bfloat16),
            jax.ShapeDtypeStruct((2 * HEADS, BLOCK, HEAD_DIM), jnp.bfloat16),
        ],
        in_specs=[LEFT] * 3,
        out_specs=[LEFT] * 2,
        scratch_shapes=[pltpu.VMEM(array.shape, array.dtype) for array in arrays]
        + [pltpu.SemaphoreType.DMA((3,)), pltpu.SemaphoreType.DMA((4 * HEADS,))],
        compiler_params=pltpu.CompilerParams(vmem_limit_bytes=56 << 20),
        name="pack",
    )(*arrays)


def pick_kernel(where, rows, above, kinds, *refs):
    outs, (buffer, sems) = refs[:GLOBALS], refs[GLOBALS:]
    group, last = row_of(where, PLANE // 2 - 1, 1)
    copies, present = [], []
    for step in range(GLOBALS):
        slot = (where[3] + step) % GLOBALS
        place = jnp.maximum(rows[group, last, WSEL + slot], above[slot]) - where[1]
        held = (place >= 0) & (place < PLANE)
        place = jnp.where(held, place, 0)
        source = kinds.at[place // 2, place % 2]
        copies.append(pltpu.make_async_copy(source, buffer.at[step], sems.at[step]))
        present.append(held)
    for copy in copies:
        copy.start()
    for step in range(GLOBALS):
        copies[step].wait()
        block = buffer[step]
        outs[step][...] = jnp.where(present[step], block, jnp.zeros_like(block))


def pick_globals(where, rows, above, kinds):
    return pl.pallas_call(
        pick_kernel,
        out_shape=[jax.ShapeDtypeStruct((BLOCK, HEAD_DIM), jnp.bfloat16)] * GLOBALS,
        in_specs=[SCALARS, SCALARS, SCALARS, LEFT],
        out_specs=[WHOLE] * GLOBALS,
        scratch_shapes=[
            pltpu.VMEM((GLOBALS, BLOCK, HEAD_DIM), jnp.bfloat16),
            pltpu.SemaphoreType.DMA((GLOBALS,)),
        ],
        compiler_params=pltpu.CompilerParams(vmem_limit_bytes=12 << 20),
        name="pick_globals",
    )(where, rows, above, kinds)


def row_of(where, at, core):
    row = 2 * at + core
    return (where[2] + 4 - row // CHUNK) % 4, row % CHUNK


def two_blocks(blocks, one, two):
    return jnp.concatenate([blocks[one // 2, one % 2], blocks[two // 2, two % 2]], axis=0)


def attend_kernel(
    where, rows, query, own, other, halo_own, halo_other, global_own, global_other,
    out, keys, values, scores, weights, sems,
):
    core, first = where[0], where[1]
    chunks = PLANE // CHUNK
    global_at = PLANE + WIN

    def copies(own_to, other_to, at):
        if at < chunks:
            target = pl.ds(at * CHUNK // 2, CHUNK // 2)
            pairs = [(own.at[target], own_to), (other.at[target], other_to)]
        elif at == chunks:
            target = pl.ds(PLANE // 2, WIN // 2)
            pairs = [(halo_own, own_to), (halo_other, other_to)]
        else:
            target = pl.ds(global_at // 2, GLOBALS // 2)
            pairs = [(global_own, own_to), (global_other, other_to)]
        for kind, (array, to) in enumerate(pairs):
            yield pltpu.make_async_copy(array, to.at[target], sems.at[kind, at])

    needed = {0: [0, chunks, chunks + 1]}
    for part in range(1, chunks):
        needed.setdefault(part * CHUNK // (2 * UNROLL), []).append(part)
    parts = [part for step in sorted(needed) for part in needed[step]]

    @pl.when(core == 0)
    def _():
        for part in parts:
            for copy in copies(keys, values, part):
                copy.start()

    @pl.when(core != 0)
    def _():
        for part in parts:
            for copy in copies(values, keys, part):
                copy.start()

    causal = lax.broadcasted_iota(jnp.int32, (BLOCK, BLOCK), 0) >= lax.broadcasted_iota(
        jnp.int32, (BLOCK, BLOCK), 1
    )

    def place_of(at, slot):
        group, row = row_of(where, at, core)
        block_id = rows[group, row, slot]
        if slot < WSEL:
            place = block_id - first
            place = jnp.where(place >= 0, place, place + PLANE + WIN)
        else:
            place = global_at + (where[3] + SLOTS - slot) % GLOBALS
        return jnp.where(block_id >= 0, place, 0), block_id >= 0

    def score_phase(at, lane):
        block_query = query[at]
        highest = None
        for slot in range(0, SLOTS, 2):
            one, listed_one = place_of(at, slot)
            two, listed_two = place_of(at, slot + 1)
            both = lax.dot_general(
                block_query, two_blocks(keys, one, two), (((1,), (1,)), ((), ())),
                preferred_element_type=jnp.float32,
            )
            for part, listed in enumerate([listed_one, listed_two]):
                score = both[:, part * BLOCK : (part + 1) * BLOCK]
                if slot + part == 0:
                    score = jnp.where(causal, score, -1e30)
                else:
                    score = jnp.where(listed, score, -1e30)
                scores[lane, slot + part] = score
                highest = score if highest is None else jnp.maximum(highest, score)
        row_max = jnp.max(highest, axis=1, keepdims=True) * FACTOR
        return jnp.broadcast_to(row_max, (BLOCK, BLOCK))

    def weight_phase(lane, row_max):
        total = None
        for slot in range(SLOTS):
            weight = jnp.exp2(scores[lane, slot] * FACTOR - row_max)
            total = weight if total is None else total + weight
            weights[lane, :, slot * BLOCK : (slot + 1) * BLOCK] = weight.astype(jnp.bfloat16)
        return jnp.sum(total, axis=1, keepdims=True)

    def value_phase(at, lane, denom):
        mixed = None
        for slot in range(0, SLOTS, 2):
            one, two = place_of(at, slot)[0], place_of(at, slot + 1)[0]
            term = jnp.dot(
                weights[lane, :, slot * BLOCK : (slot + 2) * BLOCK],
                two_blocks(values, one, two),
                preferred_element_type=jnp.float32,
            )
            mixed = term if mixed is None else mixed + term
        out[at] = (mixed / denom).astype(jnp.bfloat16)

    def step(at, carry):
        for when, needs in needed.items():

            @pl.when(at == when)
            def _(needs=needs):
                for part in needs:
                    for copy in copies(keys, values, part):
                        copy.wait()

        at = at * UNROLL
        row_max, denom = score_phase(at, 0), None
        for lane in range(UNROLL):
            following = score_phase(at + lane + 1, lane + 1) if lane + 1 < UNROLL else None
            found = weight_phase(lane, row_max)
            if lane:
                value_phase(at + lane - 1, lane - 1, denom)
            row_max, denom = following, found
        value_phase(at + UNROLL - 1, UNROLL - 1, denom)
        return carry

    lax.fori_loop(0, query.shape[0] // UNROLL, step, 0)


def attend(where, rows, query, *blocks):
    span = PLANE + WIN + GLOBALS
    pairs = query.shape[0] * SLOTS * BLOCK * BLOCK
    return pl.pallas_call(
        attend_kernel,
        out_shape=jax.ShapeDtypeStruct(query.shape, jnp.bfloat16),
        in_specs=[SCALARS, SCALARS, WHOLE] + [LEFT] * len(blocks),
        out_specs=WHOLE,
        scratch_shapes=[
            pltpu.VMEM((span // 2, 2, BLOCK, HEAD_DIM), jnp.bfloat16),
            pltpu.VMEM((span // 2, 2, BLOCK, HEAD_DIM), jnp.bfloat16),
            pltpu.VMEM((UNROLL, SLOTS, BLOCK, BLOCK), jnp.float32),
            pltpu.VMEM((UNROLL, BLOCK, SLOTS * BLOCK), jnp.bfloat16),
            pltpu.SemaphoreType.DMA((2, PLANE // CHUNK + 2)),
        ],
        compiler_params=pltpu.CompilerParams(vmem_limit_bytes=24 << 20),
        cost_estimate=pl.CostEstimate(
            flops=4 * pairs * HEAD_DIM, bytes_accessed=8 << 20, transcendentals=pairs
        ),
        name="attend",
    )(where, rows, query, *blocks)


def swapped(value):
    return lax.ppermute(value, "core", [(0, 1), (1, 0)])


def added(*values):
    return sum(value.astype(jnp.float32) for value in values).astype(jnp.bfloat16)


def shards(queries, key_vectors, value_vectors, key_blocks):
    depth = lax.axis_size("z")
    breadth = lax.axis_size("y")
    up = [(at, at + 1) for at in range(depth - 1)]
    down = [(at + 1, at) for at in range(depth - 1)]
    level = lax.axis_index("z")
    where = jnp.stack(
        [lax.axis_index("core"), level * PLANE, lax.axis_index("y"), level % GLOBALS]
    )

    kinds, sent = pack(queries, key_vectors, value_vectors)
    own = lax.all_to_all(kinds, PLANE_AXES, 0, 0, tiled=True)

    rows = jnp.stack(
        [key_blocks]
        + [
            lax.ppermute(key_blocks, "y", [(at, (at + step) % breadth) for at in range(breadth)])
            for step in range(1, breadth)
        ]
    )
    above = lax.ppermute(key_blocks[-1, WSEL:], "z", down)
    own, rows, above = lax.optimization_barrier((own, rows, above))
    query = lax.all_to_all(sent, PLANE_AXES, 0, 0, tiled=True)
    other = swapped(own)

    def within(step):
        return [(at, at - at % GLOBALS + (at + step) % GLOBALS) for at in range(depth)]

    def across(step):
        return [(at, (at + GLOBALS * step) % depth) for at in range(depth)]

    parts = pick_globals(where, rows, above, own)
    last, mine = lax.optimization_barrier((own[-WIN // 2 :], parts[0]))
    held = added(
        mine, *[lax.ppermute(parts[step], "z", within(step)) for step in range(1, GLOBALS)]
    )
    halo_own = lax.ppermute(last, "z", up)
    held = added(
        held, *[lax.ppermute(held, "z", across(step)) for step in range(1, depth // GLOBALS)]
    )
    halo_own, held = lax.optimization_barrier((halo_own, held))
    shared = [lax.ppermute(held, "z", within(step)) for step in range(1, GLOBALS)]
    halo_other = swapped(halo_own)
    global_own = jnp.stack([held] + shared).reshape(GLOBALS // 2, 2, BLOCK, HEAD_DIM)
    global_other = swapped(global_own)
    context = attend(
        where, rows, query, own, other, halo_own, halo_other, global_own, global_other
    )
    back = lax.all_to_all(context, PLANE_AXES, 0, 0, tiled=True)
    return jnp.transpose(
        back.reshape(HEADS, 2, BLOCK, HEAD_DIM), (1, 2, 0, 3)
    ).reshape(queries.shape)


def solution(mesh):
    fine = Mesh(mesh.devices.reshape(-1, 4, 4, 2), ("z",) + PLANE_AXES)
    tokens = P(("z",) + PLANE_AXES, None)
    return jax.shard_map(
        shards,
        mesh=fine,
        in_specs=(tokens, tokens, tokens, P(("z", "y"), None)),
        out_specs=tokens,
        check_vma=False,
    )
```

```python
import functools
import math

import jax
import jax.numpy as jnp
from jax import lax
from jax.experimental import pallas as pl
from jax.experimental.pallas import tpu as pltpu
from jax.sharding import Mesh
from jax.sharding import PartitionSpec as P

HEAD_DIM = 128
BLOCK = 128
WIN = 16
WSEL = 10
GLOBALS = 4
SLOTS = WSEL + GLOBALS
HEADS = 16
PLANE = 64
CHUNK = 16
FACTOR = math.log2(math.e) / math.sqrt(HEAD_DIM)
UNROLL = 4
PLANE_AXES = ("y", "x", "core")

SCALARS = pl.BlockSpec(memory_space=pltpu.SMEM)
WHOLE = pl.BlockSpec(memory_space=pltpu.VMEM)
LEFT = pl.BlockSpec(memory_space=pl.ANY)


def pack_kernel(queries, keys, values, out, query_buf, key_buf, value_buf, arrived, sems):
    def moves():
        for head in range(HEADS):
            columns = pl.ds(head * HEAD_DIM, HEAD_DIM)
            yield 0, key_buf.at[:, :, columns], out.at[2 * head, pl.ds(0, 2)]
            yield 1, value_buf.at[:, :, columns], out.at[2 * head + 1, pl.ds(0, 2)]
            yield 2, query_buf.at[0, :, columns], out.at[2 * head, 2]
            yield 2, query_buf.at[1, :, columns], out.at[2 * head + 1, 2]

    loads = [
        pltpu.make_async_copy(source, target, arrived.at[at])
        for at, (source, target) in enumerate(
            [(keys, key_buf), (values, value_buf), (queries, query_buf)]
        )
    ]
    stores = [
        (array, pltpu.make_async_copy(source, target, sems.at[at]))
        for at, (array, source, target) in enumerate(moves())
    ]
    for load in loads:
        load.start()
    for at, load in enumerate(loads):
        load.wait()
        for array, store in stores:
            if array == at:
                store.start()
    for _, store in stores:
        store.wait()


def pack(*arrays):
    arrays = [array.reshape(2, BLOCK, HEADS * HEAD_DIM) for array in arrays]
    return pl.pallas_call(
        pack_kernel,
        out_shape=jax.ShapeDtypeStruct((2 * HEADS, 3, BLOCK, HEAD_DIM), jnp.bfloat16),
        in_specs=[LEFT] * 3,
        out_specs=LEFT,
        scratch_shapes=[pltpu.VMEM(array.shape, array.dtype) for array in arrays]
        + [pltpu.SemaphoreType.DMA((3,)), pltpu.SemaphoreType.DMA((4 * HEADS,))],
        compiler_params=pltpu.CompilerParams(vmem_limit_bytes=56 << 20),
        name="pack",
    )(*arrays)


def pick_kernel(where, rows, above, kinds, out, buffer, sems):
    group, last = row_of(where, PLANE // 2 - 1, 1)
    copies, present = [], []
    for slot in range(GLOBALS):
        place = jnp.maximum(rows[group, last, WSEL + slot], above[slot]) - where[1]
        held = (place >= 0) & (place < PLANE)
        place = jnp.where(held, place, 0)
        source = kinds.at[place // 2, place % 2]
        copies.append(pltpu.make_async_copy(source, buffer.at[slot], sems.at[slot]))
        present.append(held)
    for copy in copies:
        copy.start()
    for slot in range(GLOBALS):
        copies[slot].wait()
        block = buffer[slot]
        out[slot] = jnp.where(present[slot], block, jnp.zeros_like(block))


def pick_globals(where, rows, above, kinds):
    return pl.pallas_call(
        pick_kernel,
        out_shape=jax.ShapeDtypeStruct((GLOBALS, BLOCK, HEAD_DIM), jnp.bfloat16),
        in_specs=[SCALARS, SCALARS, SCALARS, LEFT],
        out_specs=WHOLE,
        scratch_shapes=[
            pltpu.VMEM((GLOBALS, BLOCK, HEAD_DIM), jnp.bfloat16),
            pltpu.SemaphoreType.DMA((GLOBALS,)),
        ],
        compiler_params=pltpu.CompilerParams(vmem_limit_bytes=12 << 20),
        name="pick_globals",
    )(where, rows, above, kinds)


def row_of(where, at, core):
    row = 2 * at + core
    return (where[2] + 4 - row // CHUNK) % 4, row % CHUNK


def two_blocks(blocks, one, two):
    return jnp.concatenate([blocks[one // 2, one % 2], blocks[two // 2, two % 2]], axis=0)


def attend_kernel(start, high, kept, where, rows, own, other, global_own, global_other, *refs):
    if kept:
        halo_own, halo_other, before, *refs = refs
    out, keys, values, scores, weights, sems = refs
    core, first = where[0], where[1]
    chunks = high // CHUNK
    halo_at = high
    global_at = high + (WIN if kept else 0)
    count = kept if kept else out.shape[0]

    def copies(own_to, other_to, at):
        if at < chunks:
            source = pl.ds(at * CHUNK // 2, CHUNK // 2)
            pairs = [(own.at[source, pl.ds(0, 2)], own_to), (other.at[source, pl.ds(0, 2)], other_to)]
            target = source
        elif at == chunks:
            pairs = [(global_own, own_to), (global_other, other_to)]
            target = pl.ds(global_at // 2, GLOBALS // 2)
        else:
            pairs = [(halo_own, own_to), (halo_other, other_to)]
            target = pl.ds(halo_at // 2, WIN // 2)
        for kind, (array, to) in enumerate(pairs):
            yield pltpu.make_async_copy(array, to.at[target], sems.at[kind, at])

    parts = list(range(chunks + (2 if kept else 1)))

    @pl.when(core == 0)
    def _():
        for part in parts:
            for copy in copies(keys, values, part):
                copy.start()

    @pl.when(core != 0)
    def _():
        for part in parts:
            for copy in copies(values, keys, part):
                copy.start()

    if kept:
        out[kept:] = before[...]

    needed = {}
    for part in parts:
        step = 0
        if part < chunks:
            step = max(0, (part * CHUNK - 2 * start) // (2 * UNROLL))
        needed.setdefault(step, []).append(part)

    causal = lax.broadcasted_iota(jnp.int32, (BLOCK, BLOCK), 0) >= lax.broadcasted_iota(
        jnp.int32, (BLOCK, BLOCK), 1
    )

    def place_of(at, slot):
        group, row = row_of(where, start + at, core)
        block_id = rows[group, row, slot]
        if slot < WSEL:
            place = block_id - first
            if kept:
                place = jnp.where(place >= 0, place, place + halo_at + WIN)
        else:
            place = global_at + slot - WSEL
        return jnp.where(block_id >= 0, place, 0), block_id >= 0

    def score_phase(at, lane):
        block_query = own[start + at, 2]
        highest = None
        for slot in range(0, SLOTS, 2):
            one, listed_one = place_of(at, slot)
            two, listed_two = place_of(at, slot + 1)
            both = lax.dot_general(
                block_query, two_blocks(keys, one, two), (((1,), (1,)), ((), ())),
                preferred_element_type=jnp.float32,
            )
            for part, listed in enumerate([listed_one, listed_two]):
                score = both[:, part * BLOCK : (part + 1) * BLOCK]
                if slot + part == 0:
                    score = jnp.where(causal, score, -1e30)
                elif kept or slot + part >= WSEL:
                    score = jnp.where(listed, score, -1e30)
                scores[lane, slot + part] = score
                highest = score if highest is None else jnp.maximum(highest, score)
        row_max = jnp.max(highest, axis=1, keepdims=True) * FACTOR
        return jnp.broadcast_to(row_max, (BLOCK, BLOCK))

    def weight_phase(lane, row_max):
        total = None
        for slot in range(SLOTS):
            weight = jnp.exp2(scores[lane, slot] * FACTOR - row_max)
            total = weight if total is None else total + weight
            weights[lane, :, slot * BLOCK : (slot + 1) * BLOCK] = weight.astype(jnp.bfloat16)
        return jnp.sum(total, axis=1, keepdims=True)

    def value_phase(at, lane, denom):
        mixed = None
        for slot in range(0, SLOTS, 2):
            one, two = place_of(at, slot)[0], place_of(at, slot + 1)[0]
            term = jnp.dot(
                weights[lane, :, slot * BLOCK : (slot + 2) * BLOCK],
                two_blocks(values, one, two),
                preferred_element_type=jnp.float32,
            )
            mixed = term if mixed is None else mixed + term
        out[at] = (mixed / denom).astype(jnp.bfloat16)

    def step(at, carry):
        for when, needs in needed.items():

            @pl.when(at == when)
            def _(needs=needs):
                for part in needs:
                    for copy in copies(keys, values, part):
                        copy.wait()

        at = at * UNROLL
        row_max, denom = score_phase(at, 0), None
        for lane in range(UNROLL):
            following = score_phase(at + lane + 1, lane + 1) if lane + 1 < UNROLL else None
            found = weight_phase(lane, row_max)
            if lane:
                value_phase(at + lane - 1, lane - 1, denom)
            row_max, denom = following, found
        value_phase(at + UNROLL - 1, UNROLL - 1, denom)
        return carry

    lax.fori_loop(0, count // UNROLL, step, 0)


def attend(start, high, where, rows, own, other, global_own, global_other, *halo):
    total = own.shape[0] - start
    kept = total - halo[-1].shape[0] if halo else 0
    count = kept if kept else total
    span = high + GLOBALS + (WIN if kept else 0)
    pairs = count * SLOTS * BLOCK * BLOCK
    return pl.pallas_call(
        functools.partial(attend_kernel, start, high, kept),
        out_shape=jax.ShapeDtypeStruct((total, BLOCK, HEAD_DIM), jnp.bfloat16),
        in_specs=[SCALARS, SCALARS, WHOLE]
        + [LEFT] * 3
        + ([LEFT, LEFT, WHOLE] if kept else []),
        out_specs=WHOLE,
        scratch_shapes=[
            pltpu.VMEM((span // 2, 2, BLOCK, HEAD_DIM), jnp.bfloat16),
            pltpu.VMEM((span // 2, 2, BLOCK, HEAD_DIM), jnp.bfloat16),
            pltpu.VMEM((UNROLL, SLOTS, BLOCK, BLOCK), jnp.float32),
            pltpu.VMEM((UNROLL, BLOCK, SLOTS * BLOCK), jnp.bfloat16),
            pltpu.SemaphoreType.DMA((2, high // CHUNK + 2)),
        ],
        compiler_params=pltpu.CompilerParams(vmem_limit_bytes=24 << 20),
        cost_estimate=pl.CostEstimate(
            flops=4 * pairs * HEAD_DIM, bytes_accessed=8 << 20, transcendentals=pairs
        ),
        name="attend_first" if kept else "attend_rest",
    )(where, rows, own, other, global_own, global_other, *halo)


def swapped(value):
    return lax.ppermute(value, "core", [(0, 1), (1, 0)])


def shards(queries, key_vectors, value_vectors, key_blocks):
    depth = lax.axis_size("z")
    breadth = lax.axis_size("y")
    up = [(at, at + 1) for at in range(depth - 1)]
    down = [(at + 1, at) for at in range(depth - 1)]
    where = jnp.stack(
        [lax.axis_index("core"), lax.axis_index("z") * PLANE, lax.axis_index("y")]
    )

    received = lax.all_to_all(
        pack(queries, key_vectors, value_vectors), PLANE_AXES, 0, 0, tiled=True
    )

    rows = jnp.stack(
        [key_blocks]
        + [
            lax.ppermute(key_blocks, "y", [(at, (at + step) % breadth) for at in range(breadth)])
            for step in range(1, breadth)
        ]
    )
    above = lax.ppermute(key_blocks[-1, WSEL:], "z", down)
    own, rows, above = lax.optimization_barrier((received, rows, above))
    other = swapped(own)

    part = pick_globals(where, rows, above, own).reshape(depth, -1, HEAD_DIM)
    pieces = lax.all_to_all(part, "z", 0, 0, tiled=True)
    summed = jnp.sum(pieces.astype(jnp.float32), axis=0, keepdims=True).astype(jnp.bfloat16)
    global_own = lax.all_to_all(jnp.broadcast_to(summed, part.shape), "z", 0, 0, tiled=True)
    last, global_own = lax.optimization_barrier((own[-WIN // 2 :, :2], global_own))
    pair = (GLOBALS // 2, 2, BLOCK, HEAD_DIM)
    global_own = global_own.reshape(pair)
    global_other = swapped(global_own)
    halo_own = lax.ppermute(last, "z", up)
    rest = attend(
        WIN // 2, PLANE, where, rows, own, other, global_own, global_other
    )
    rest, halo_own = lax.optimization_barrier((rest, halo_own))
    context = attend(
        0, CHUNK, where, rows, own, other, global_own, global_other,
        halo_own, swapped(halo_own), rest,
    )
    back = lax.all_to_all(context, PLANE_AXES, 0, 0, tiled=True)
    return jnp.transpose(
        back.reshape(HEADS, 2, BLOCK, HEAD_DIM), (1, 2, 0, 3)
    ).reshape(queries.shape)


def solution(mesh):
    fine = Mesh(mesh.devices.reshape(-1, 4, 4, 2), ("z",) + PLANE_AXES)
    tokens = P(("z",) + PLANE_AXES, None)
    return jax.shard_map(
        shards,
        mesh=fine,
        in_specs=(tokens, tokens, tokens, P(("z", "y"), None)),
        out_specs=tokens,
        check_vma=False,
    )
```

```python
import functools
import math

import jax
import jax.numpy as jnp
from jax import lax
from jax.experimental import pallas as pl
from jax.experimental.pallas import tpu as pltpu
from jax.sharding import Mesh
from jax.sharding import PartitionSpec as P

HEAD_DIM = 128
BLOCK = 128
WIN = 16
WSEL = 10
GLOBALS = 4
SLOTS = WSEL + GLOBALS
HEADS = 16
PLANE = 64
CHUNK = 16
FACTOR = math.log2(math.e) / math.sqrt(HEAD_DIM)
UNROLL = 4
PLANE_AXES = ("y", "x", "core")

SCALARS = pl.BlockSpec(memory_space=pltpu.SMEM)
WHOLE = pl.BlockSpec(memory_space=pltpu.VMEM)
LEFT = pl.BlockSpec(memory_space=pl.ANY)


def pack_kernel(queries, keys, values, out, query_buf, key_buf, value_buf, arrived, sems):
    def moves():
        for head in range(HEADS):
            columns = pl.ds(head * HEAD_DIM, HEAD_DIM)
            yield 0, key_buf.at[:, :, columns], out.at[2 * head, pl.ds(0, 2)]
            yield 1, value_buf.at[:, :, columns], out.at[2 * head + 1, pl.ds(0, 2)]
            yield 2, query_buf.at[0, :, columns], out.at[2 * head, 2]
            yield 2, query_buf.at[1, :, columns], out.at[2 * head + 1, 2]

    loads = [
        pltpu.make_async_copy(source, target, arrived.at[at])
        for at, (source, target) in enumerate(
            [(keys, key_buf), (values, value_buf), (queries, query_buf)]
        )
    ]
    stores = [
        (array, pltpu.make_async_copy(source, target, sems.at[at]))
        for at, (array, source, target) in enumerate(moves())
    ]
    for load in loads:
        load.start()
    for at, load in enumerate(loads):
        load.wait()
        for array, store in stores:
            if array == at:
                store.start()
    for _, store in stores:
        store.wait()


def pack(*arrays):
    arrays = [array.reshape(2, BLOCK, HEADS * HEAD_DIM) for array in arrays]
    return pl.pallas_call(
        pack_kernel,
        out_shape=jax.ShapeDtypeStruct((2 * HEADS, 3, BLOCK, HEAD_DIM), jnp.bfloat16),
        in_specs=[LEFT] * 3,
        out_specs=LEFT,
        scratch_shapes=[pltpu.VMEM(array.shape, array.dtype) for array in arrays]
        + [pltpu.SemaphoreType.DMA((3,)), pltpu.SemaphoreType.DMA((4 * HEADS,))],
        compiler_params=pltpu.CompilerParams(vmem_limit_bytes=56 << 20),
        name="pack",
    )(*arrays)


def early_kernel(ids, base, keys, values, out, key_buf, value_buf, arrived, sems):
    even = ids[0] == base[0]
    for slot in range(1, GLOBALS):
        even = even | (ids[slot] == base[0])
    which = jnp.where(even, 0, 1)
    loads = [
        pltpu.make_async_copy(keys.at[which], key_buf, arrived.at[0]),
        pltpu.make_async_copy(values.at[which], value_buf, arrived.at[1]),
    ]
    stores = [[], []]
    for head in range(HEADS):
        columns = pl.ds(head * HEAD_DIM, HEAD_DIM)
        for kind, buf in enumerate([key_buf, value_buf]):
            stores[kind].append(
                pltpu.make_async_copy(
                    buf.at[:, columns], out.at[2 * head + kind], sems.at[kind, head]
                )
            )
    for load in loads:
        load.start()
    for load, each in zip(loads, stores):
        load.wait()
        for store in each:
            store.start()
    for each in stores:
        for store in each:
            store.wait()


def pack_early(ids, base, *arrays):
    arrays = [array.reshape(2, BLOCK, HEADS * HEAD_DIM) for array in arrays]
    return pl.pallas_call(
        early_kernel,
        out_shape=jax.ShapeDtypeStruct((2 * HEADS, BLOCK, HEAD_DIM), jnp.bfloat16),
        in_specs=[SCALARS, SCALARS, LEFT, LEFT],
        out_specs=LEFT,
        scratch_shapes=[pltpu.VMEM(array.shape[1:], array.dtype) for array in arrays]
        + [pltpu.SemaphoreType.DMA((2,)), pltpu.SemaphoreType.DMA((2, HEADS))],
        compiler_params=pltpu.CompilerParams(vmem_limit_bytes=56 << 20),
        name="pack_early",
    )(ids, base, *arrays)


def early_pick_kernel(where, rows, above, kinds, *refs):
    outs, (buffer, sems) = refs[:GLOBALS], refs[GLOBALS:]
    group, last = row_of(where, PLANE // 2 - 1, 1)
    copies, present, sources = [], [], []
    for step in range(GLOBALS):
        slot = (where[3] + step) % GLOBALS
        place = jnp.maximum(rows[group, last, WSEL + slot], above[slot]) - where[1]
        held = (place >= 0) & (place < PLANE)
        source = jnp.where(held, place, 0) // 2
        copies.append(pltpu.make_async_copy(kinds.at[source], buffer.at[step], sems.at[step]))
        present.append(held)
        sources.append(jnp.where(held, source, -1 - step))
    for copy in copies:
        copy.start()
    clash = jnp.int32(0)
    for one in range(GLOBALS):
        for two in range(one):
            clash = jnp.where(sources[one] == sources[two], 1, clash)
    for step in range(GLOBALS):
        copies[step].wait()
        block = buffer[step]
        outs[step][:BLOCK] = jnp.where(present[step], block, jnp.zeros_like(block))
        flag = jnp.where(clash > 0, 1.0, 0.0)
        outs[step][BLOCK:] = jnp.full((16, HEAD_DIM), flag, jnp.float32).astype(jnp.bfloat16)


def pick_early(where, rows, above, kinds):
    return pl.pallas_call(
        early_pick_kernel,
        out_shape=[jax.ShapeDtypeStruct((BLOCK + 16, HEAD_DIM), jnp.bfloat16)] * GLOBALS,
        in_specs=[SCALARS, SCALARS, SCALARS, LEFT],
        out_specs=[WHOLE] * GLOBALS,
        scratch_shapes=[
            pltpu.VMEM((GLOBALS, BLOCK, HEAD_DIM), jnp.bfloat16),
            pltpu.SemaphoreType.DMA((GLOBALS,)),
        ],
        compiler_params=pltpu.CompilerParams(vmem_limit_bytes=12 << 20),
        name="pick_early",
    )(where, rows, above, kinds)


def pick_kernel(where, rows, above, kinds, out, buffer, sems):
    group, last = row_of(where, PLANE // 2 - 1, 1)
    copies, present = [], []
    for slot in range(GLOBALS):
        place = jnp.maximum(rows[group, last, WSEL + slot], above[slot]) - where[1]
        held = (place >= 0) & (place < PLANE)
        place = jnp.where(held, place, 0)
        source = kinds.at[place // 2, place % 2]
        copies.append(pltpu.make_async_copy(source, buffer.at[slot], sems.at[slot]))
        present.append(held)
    for copy in copies:
        copy.start()
    for slot in range(GLOBALS):
        copies[slot].wait()
        block = buffer[slot]
        out[slot] = jnp.where(present[slot], block, jnp.zeros_like(block))


def pick_globals(where, rows, above, kinds):
    return pl.pallas_call(
        pick_kernel,
        out_shape=jax.ShapeDtypeStruct((GLOBALS, BLOCK, HEAD_DIM), jnp.bfloat16),
        in_specs=[SCALARS, SCALARS, SCALARS, LEFT],
        out_specs=WHOLE,
        scratch_shapes=[
            pltpu.VMEM((GLOBALS, BLOCK, HEAD_DIM), jnp.bfloat16),
            pltpu.SemaphoreType.DMA((GLOBALS,)),
        ],
        compiler_params=pltpu.CompilerParams(vmem_limit_bytes=12 << 20),
        name="pick_globals",
    )(where, rows, above, kinds)


def row_of(where, at, core):
    row = 2 * at + core
    return (where[2] + 4 - row // CHUNK) % 4, row % CHUNK


def two_blocks(blocks, one, two):
    return jnp.concatenate([blocks[one // 2, one % 2], blocks[two // 2, two % 2]], axis=0)


def attend_kernel(start, high, kept, where, rows, own, other, global_own, global_other, *refs):
    if kept:
        halo_own, halo_other, before, *refs = refs
    out, keys, values, scores, weights, sems = refs
    core, first = where[0], where[1]
    chunks = high // CHUNK
    halo_at = high
    global_at = high + (WIN if kept else 0)
    count = kept if kept else out.shape[0]

    def copies(own_to, other_to, at):
        if at < chunks:
            source = pl.ds(at * CHUNK // 2, CHUNK // 2)
            pairs = [(own.at[source, pl.ds(0, 2)], own_to), (other.at[source, pl.ds(0, 2)], other_to)]
            target = source
        elif at == chunks:
            pairs = [(global_own, own_to), (global_other, other_to)]
            target = pl.ds(global_at // 2, GLOBALS // 2)
        else:
            pairs = [(halo_own, own_to), (halo_other, other_to)]
            target = pl.ds(halo_at // 2, WIN // 2)
        for kind, (array, to) in enumerate(pairs):
            yield pltpu.make_async_copy(array, to.at[target], sems.at[kind, at])

    parts = list(range(chunks + (2 if kept else 1)))

    @pl.when(core == 0)
    def _():
        for part in parts:
            for copy in copies(keys, values, part):
                copy.start()

    @pl.when(core != 0)
    def _():
        for part in parts:
            for copy in copies(values, keys, part):
                copy.start()

    if kept:
        out[kept:] = before[...]

    needed = {}
    for part in parts:
        step = 0
        if part < chunks:
            step = max(0, (part * CHUNK - 2 * start) // (2 * UNROLL))
        needed.setdefault(step, []).append(part)

    causal = lax.broadcasted_iota(jnp.int32, (BLOCK, BLOCK), 0) >= lax.broadcasted_iota(
        jnp.int32, (BLOCK, BLOCK), 1
    )

    def place_of(at, slot):
        group, row = row_of(where, start + at, core)
        block_id = rows[group, row, slot]
        if slot < WSEL:
            place = block_id - first
            if kept:
                place = jnp.where(place >= 0, place, place + halo_at + WIN)
        else:
            place = global_at + (where[3] + SLOTS - slot) % GLOBALS
        return jnp.where(block_id >= 0, place, 0), block_id >= 0

    def score_phase(at, lane):
        block_query = own[start + at, 2]
        highest = None
        for slot in range(0, SLOTS, 2):
            one, listed_one = place_of(at, slot)
            two, listed_two = place_of(at, slot + 1)
            both = lax.dot_general(
                block_query, two_blocks(keys, one, two), (((1,), (1,)), ((), ())),
                preferred_element_type=jnp.float32,
            )
            for part, listed in enumerate([listed_one, listed_two]):
                score = both[:, part * BLOCK : (part + 1) * BLOCK]
                if slot + part == 0:
                    score = jnp.where(causal, score, -1e30)
                elif kept or slot + part >= WSEL:
                    score = jnp.where(listed, score, -1e30)
                scores[lane, slot + part] = score
                highest = score if highest is None else jnp.maximum(highest, score)
        row_max = jnp.max(highest, axis=1, keepdims=True) * FACTOR
        return jnp.broadcast_to(row_max, (BLOCK, BLOCK))

    def weight_phase(lane, row_max):
        total = None
        for slot in range(SLOTS):
            weight = jnp.exp2(scores[lane, slot] * FACTOR - row_max)
            total = weight if total is None else total + weight
            weights[lane, :, slot * BLOCK : (slot + 1) * BLOCK] = weight.astype(jnp.bfloat16)
        return jnp.sum(total, axis=1, keepdims=True)

    def value_phase(at, lane, denom):
        mixed = None
        for slot in range(0, SLOTS, 2):
            one, two = place_of(at, slot)[0], place_of(at, slot + 1)[0]
            term = jnp.dot(
                weights[lane, :, slot * BLOCK : (slot + 2) * BLOCK],
                two_blocks(values, one, two),
                preferred_element_type=jnp.float32,
            )
            mixed = term if mixed is None else mixed + term
        out[at] = (mixed / denom).astype(jnp.bfloat16)

    def step(at, carry):
        for when, needs in needed.items():

            @pl.when(at == when)
            def _(needs=needs):
                for part in needs:
                    for copy in copies(keys, values, part):
                        copy.wait()

        at = at * UNROLL
        row_max, denom = score_phase(at, 0), None
        for lane in range(UNROLL):
            following = score_phase(at + lane + 1, lane + 1) if lane + 1 < UNROLL else None
            found = weight_phase(lane, row_max)
            if lane:
                value_phase(at + lane - 1, lane - 1, denom)
            row_max, denom = following, found
        value_phase(at + UNROLL - 1, UNROLL - 1, denom)
        return carry

    lax.fori_loop(0, count // UNROLL, step, 0)


def attend(start, high, where, rows, own, other, global_own, global_other, *halo):
    total = own.shape[0] - start
    kept = total - halo[-1].shape[0] if halo else 0
    count = kept if kept else total
    span = high + GLOBALS + (WIN if kept else 0)
    pairs = count * SLOTS * BLOCK * BLOCK
    return pl.pallas_call(
        functools.partial(attend_kernel, start, high, kept),
        out_shape=jax.ShapeDtypeStruct((total, BLOCK, HEAD_DIM), jnp.bfloat16),
        in_specs=[SCALARS, SCALARS, WHOLE]
        + [LEFT] * 3
        + ([LEFT, LEFT, WHOLE] if kept else []),
        out_specs=WHOLE,
        scratch_shapes=[
            pltpu.VMEM((span // 2, 2, BLOCK, HEAD_DIM), jnp.bfloat16),
            pltpu.VMEM((span // 2, 2, BLOCK, HEAD_DIM), jnp.bfloat16),
            pltpu.VMEM((UNROLL, SLOTS, BLOCK, BLOCK), jnp.float32),
            pltpu.VMEM((UNROLL, BLOCK, SLOTS * BLOCK), jnp.bfloat16),
            pltpu.SemaphoreType.DMA((2, high // CHUNK + 2)),
        ],
        compiler_params=pltpu.CompilerParams(vmem_limit_bytes=24 << 20),
        cost_estimate=pl.CostEstimate(
            flops=4 * pairs * HEAD_DIM, bytes_accessed=8 << 20, transcendentals=pairs
        ),
        name="attend_first" if kept else "attend_rest",
    )(where, rows, own, other, global_own, global_other, *halo)


def swapped(value):
    return lax.ppermute(value, "core", [(0, 1), (1, 0)])


def added(*values):
    return sum(value.astype(jnp.float32) for value in values).astype(jnp.bfloat16)


def shards(queries, key_vectors, value_vectors, key_blocks):
    depth = lax.axis_size("z")
    breadth = lax.axis_size("y")
    up = [(at, at + 1) for at in range(depth - 1)]
    down = [(at + 1, at) for at in range(depth - 1)]
    level, here = lax.axis_index("z"), lax.axis_index("y")
    where = jnp.stack([lax.axis_index("core"), level * PLANE, here, level % GLOBALS])

    ahead = lax.ppermute(
        key_blocks[-1, WSEL:], ("z", "y"), [(at + 1, at) for at in range(depth * breadth - 1)]
    )
    base = level * PLANE + 2 * lax.axis_index(PLANE_AXES)
    early = lax.all_to_all(
        pack_early(ahead, base[None], key_vectors, value_vectors), PLANE_AXES, 0, 0, tiled=True
    )

    rows = jnp.stack(
        [key_blocks]
        + [
            lax.ppermute(key_blocks, "y", [(at, (at + step) % breadth) for at in range(breadth)])
            for step in range(1, breadth)
        ]
    )
    above = lax.ppermute(key_blocks[-1, WSEL:], "z", down)

    packed = pack(queries, key_vectors, value_vectors)
    early, packed, rows, above = lax.optimization_barrier((early, packed, rows, above))
    own = lax.all_to_all(packed, PLANE_AXES, 0, 0, tiled=True)

    def within(step):
        return [(at, at - at % GLOBALS + (at + step) % GLOBALS) for at in range(depth)]

    def across(step):
        return [(at, (at + GLOBALS * step) % depth) for at in range(depth)]

    parts = pick_early(where, rows, above, early)
    held = added(
        parts[0], *[lax.ppermute(parts[step], "z", within(step)) for step in range(1, GLOBALS)]
    )
    held = added(
        held, *[lax.ppermute(held, "z", across(step)) for step in range(1, depth // GLOBALS)]
    )
    clash = held[BLOCK, 0].astype(jnp.float32) > 0.5
    held = held[:BLOCK]
    global_own = jnp.stack(
        [held] + [lax.ppermute(held, "z", within(step)) for step in range(1, GLOBALS)]
    )

    def again(blocks):
        part = pick_globals(where, rows, above, blocks).astype(jnp.float32)
        full = lax.psum(part, "z").astype(jnp.bfloat16)
        return full[(level + GLOBALS - jnp.arange(GLOBALS)) % GLOBALS]

    own, shared = lax.optimization_barrier((own, global_own))
    global_own = lax.cond(clash, again, lambda blocks: shared, own)
    other = swapped(own)
    pair = (GLOBALS // 2, 2, BLOCK, HEAD_DIM)
    global_own = global_own.reshape(pair)
    global_other = swapped(global_own)
    halo_own = lax.ppermute(own[-WIN // 2 :, :2], "z", up)
    rest = attend(
        WIN // 2, PLANE, where, rows, own, other, global_own, global_other
    )
    rest, halo_own = lax.optimization_barrier((rest, halo_own))
    context = attend(
        0, CHUNK, where, rows, own, other, global_own, global_other,
        halo_own, swapped(halo_own), rest,
    )
    back = lax.all_to_all(context, PLANE_AXES, 0, 0, tiled=True)
    return jnp.transpose(
        back.reshape(HEADS, 2, BLOCK, HEAD_DIM), (1, 2, 0, 3)
    ).reshape(queries.shape)


def solution(mesh):
    fine = Mesh(mesh.devices.reshape(-1, 4, 4, 2), ("z",) + PLANE_AXES)
    tokens = P(("z",) + PLANE_AXES, None)
    return jax.shard_map(
        shards,
        mesh=fine,
        in_specs=(tokens, tokens, tokens, P(("z", "y"), None)),
        out_specs=tokens,
        check_vma=False,
    )
```

```python
import functools
import math

import jax
import jax.numpy as jnp
from jax import lax
from jax.experimental import pallas as pl
from jax.experimental.pallas import tpu as pltpu
from jax.sharding import Mesh
from jax.sharding import PartitionSpec as P

HEAD_DIM = 128
BLOCK = 128
WIN = 16
WSEL = 10
GLOBALS = 4
SLOTS = WSEL + GLOBALS
HEADS = 16
PLANE = 64
CHUNK = 16
FACTOR = math.log2(math.e) / math.sqrt(HEAD_DIM)
UNROLL = 4
PLANE_AXES = ("y", "x", "core")
Z_AXES = ("far", "near")

SCALARS = pl.BlockSpec(memory_space=pltpu.SMEM)
WHOLE = pl.BlockSpec(memory_space=pltpu.VMEM)
LEFT = pl.BlockSpec(memory_space=pl.ANY)


def pack_kernel(queries, keys, values, out, query_buf, key_buf, value_buf, arrived, sems):
    def moves():
        for head in range(HEADS):
            columns = pl.ds(head * HEAD_DIM, HEAD_DIM)
            yield 0, key_buf.at[:, :, columns], out.at[2 * head, pl.ds(0, 2)]
            yield 1, value_buf.at[:, :, columns], out.at[2 * head + 1, pl.ds(0, 2)]
            yield 2, query_buf.at[0, :, columns], out.at[2 * head, 2]
            yield 2, query_buf.at[1, :, columns], out.at[2 * head + 1, 2]

    loads = [
        pltpu.make_async_copy(source, target, arrived.at[at])
        for at, (source, target) in enumerate(
            [(keys, key_buf), (values, value_buf), (queries, query_buf)]
        )
    ]
    stores = [
        (array, pltpu.make_async_copy(source, target, sems.at[at]))
        for at, (array, source, target) in enumerate(moves())
    ]
    for load in loads:
        load.start()
    for at, load in enumerate(loads):
        load.wait()
        for array, store in stores:
            if array == at:
                store.start()
    for _, store in stores:
        store.wait()


def pack(*arrays):
    arrays = [array.reshape(2, BLOCK, HEADS * HEAD_DIM) for array in arrays]
    return pl.pallas_call(
        pack_kernel,
        out_shape=jax.ShapeDtypeStruct((2 * HEADS, 3, BLOCK, HEAD_DIM), jnp.bfloat16),
        in_specs=[LEFT] * 3,
        out_specs=LEFT,
        scratch_shapes=[pltpu.VMEM(array.shape, array.dtype) for array in arrays]
        + [pltpu.SemaphoreType.DMA((3,)), pltpu.SemaphoreType.DMA((4 * HEADS,))],
        compiler_params=pltpu.CompilerParams(vmem_limit_bytes=56 << 20),
        name="pack",
    )(*arrays)


def pick_kernel(where, rows, above, kinds, out, buffer, sems):
    group, last = row_of(where, PLANE // 2 - 1, 1)
    copies, present = [], []
    for slot in range(GLOBALS):
        place = jnp.maximum(rows[group, last, WSEL + slot], above[slot]) - where[1]
        held = (place >= 0) & (place < PLANE)
        place = jnp.where(held, place, 0)
        source = kinds.at[place // 2, place % 2]
        copies.append(pltpu.make_async_copy(source, buffer.at[slot], sems.at[slot]))
        present.append(held)
    for copy in copies:
        copy.start()
    for slot in range(GLOBALS):
        copies[slot].wait()
        block = buffer[slot]
        out[slot] = jnp.where(present[slot], block, jnp.zeros_like(block))


def pick_globals(where, rows, above, kinds):
    return pl.pallas_call(
        pick_kernel,
        out_shape=jax.ShapeDtypeStruct((GLOBALS, BLOCK, HEAD_DIM), jnp.bfloat16),
        in_specs=[SCALARS, SCALARS, SCALARS, LEFT],
        out_specs=WHOLE,
        scratch_shapes=[
            pltpu.VMEM((GLOBALS, BLOCK, HEAD_DIM), jnp.bfloat16),
            pltpu.SemaphoreType.DMA((GLOBALS,)),
        ],
        compiler_params=pltpu.CompilerParams(vmem_limit_bytes=12 << 20),
        name="pick_globals",
    )(where, rows, above, kinds)


def row_of(where, at, core):
    row = 2 * at + core
    return (where[2] + 4 - row // CHUNK) % 4, row % CHUNK


def two_blocks(blocks, one, two):
    return jnp.concatenate([blocks[one // 2, one % 2], blocks[two // 2, two % 2]], axis=0)


def attend_kernel(start, high, kept, where, rows, own, other, global_own, global_other, *refs):
    if kept:
        halo_own, halo_other, before, *refs = refs
    out, keys, values, scores, weights, sems = refs
    core, first = where[0], where[1]
    chunks = high // CHUNK
    halo_at = high
    global_at = high + (WIN if kept else 0)
    count = kept if kept else out.shape[0]

    def copies(own_to, other_to, at):
        if at < chunks:
            source = pl.ds(at * CHUNK // 2, CHUNK // 2)
            pairs = [(own.at[source, pl.ds(0, 2)], own_to), (other.at[source, pl.ds(0, 2)], other_to)]
            target = source
        elif at == chunks:
            pairs = [(global_own, own_to), (global_other, other_to)]
            target = pl.ds(global_at // 2, GLOBALS // 2)
        else:
            pairs = [(halo_own, own_to), (halo_other, other_to)]
            target = pl.ds(halo_at // 2, WIN // 2)
        for kind, (array, to) in enumerate(pairs):
            yield pltpu.make_async_copy(array, to.at[target], sems.at[kind, at])

    parts = list(range(chunks + (2 if kept else 1)))

    @pl.when(core == 0)
    def _():
        for part in parts:
            for copy in copies(keys, values, part):
                copy.start()

    @pl.when(core != 0)
    def _():
        for part in parts:
            for copy in copies(values, keys, part):
                copy.start()

    if kept:
        out[kept:] = before[...]

    needed = {}
    for part in parts:
        step = 0
        if part < chunks:
            step = max(0, (part * CHUNK - 2 * start) // (2 * UNROLL))
        needed.setdefault(step, []).append(part)

    causal = lax.broadcasted_iota(jnp.int32, (BLOCK, BLOCK), 0) >= lax.broadcasted_iota(
        jnp.int32, (BLOCK, BLOCK), 1
    )

    def place_of(at, slot):
        group, row = row_of(where, start + at, core)
        block_id = rows[group, row, slot]
        if slot < WSEL:
            place = block_id - first
            if kept:
                place = jnp.where(place >= 0, place, place + halo_at + WIN)
        else:
            place = global_at + slot - WSEL
        return jnp.where(block_id >= 0, place, 0), block_id >= 0

    def score_phase(at, lane):
        block_query = own[start + at, 2]
        highest = None
        for slot in range(0, SLOTS, 2):
            one, listed_one = place_of(at, slot)
            two, listed_two = place_of(at, slot + 1)
            both = lax.dot_general(
                block_query, two_blocks(keys, one, two), (((1,), (1,)), ((), ())),
                preferred_element_type=jnp.float32,
            )
            for part, listed in enumerate([listed_one, listed_two]):
                score = both[:, part * BLOCK : (part + 1) * BLOCK]
                if slot + part == 0:
                    score = jnp.where(causal, score, -1e30)
                elif kept or slot + part >= WSEL:
                    score = jnp.where(listed, score, -1e30)
                scores[lane, slot + part] = score
                highest = score if highest is None else jnp.maximum(highest, score)
        row_max = jnp.max(highest, axis=1, keepdims=True) * FACTOR
        return jnp.broadcast_to(row_max, (BLOCK, BLOCK))

    def weight_phase(lane, row_max):
        total = None
        for slot in range(SLOTS):
            weight = jnp.exp2(scores[lane, slot] * FACTOR - row_max)
            total = weight if total is None else total + weight
            weights[lane, :, slot * BLOCK : (slot + 1) * BLOCK] = weight.astype(jnp.bfloat16)
        return jnp.sum(total, axis=1, keepdims=True)

    def value_phase(at, lane, denom):
        mixed = None
        for slot in range(0, SLOTS, 2):
            one, two = place_of(at, slot)[0], place_of(at, slot + 1)[0]
            term = jnp.dot(
                weights[lane, :, slot * BLOCK : (slot + 2) * BLOCK],
                two_blocks(values, one, two),
                preferred_element_type=jnp.float32,
            )
            mixed = term if mixed is None else mixed + term
        out[at] = (mixed / denom).astype(jnp.bfloat16)

    def step(at, carry):
        for when, needs in needed.items():

            @pl.when(at == when)
            def _(needs=needs):
                for part in needs:
                    for copy in copies(keys, values, part):
                        copy.wait()

        at = at * UNROLL
        row_max, denom = score_phase(at, 0), None
        for lane in range(UNROLL):
            following = score_phase(at + lane + 1, lane + 1) if lane + 1 < UNROLL else None
            found = weight_phase(lane, row_max)
            if lane:
                value_phase(at + lane - 1, lane - 1, denom)
            row_max, denom = following, found
        value_phase(at + UNROLL - 1, UNROLL - 1, denom)
        return carry

    lax.fori_loop(0, count // UNROLL, step, 0)


def attend(start, high, where, rows, own, other, global_own, global_other, *halo):
    total = own.shape[0] - start
    kept = total - halo[-1].shape[0] if halo else 0
    count = kept if kept else total
    span = high + GLOBALS + (WIN if kept else 0)
    pairs = count * SLOTS * BLOCK * BLOCK
    return pl.pallas_call(
        functools.partial(attend_kernel, start, high, kept),
        out_shape=jax.ShapeDtypeStruct((total, BLOCK, HEAD_DIM), jnp.bfloat16),
        in_specs=[SCALARS, SCALARS, WHOLE]
        + [LEFT] * 3
        + ([LEFT, LEFT, WHOLE] if kept else []),
        out_specs=WHOLE,
        scratch_shapes=[
            pltpu.VMEM((span // 2, 2, BLOCK, HEAD_DIM), jnp.bfloat16),
            pltpu.VMEM((span // 2, 2, BLOCK, HEAD_DIM), jnp.bfloat16),
            pltpu.VMEM((UNROLL, SLOTS, BLOCK, BLOCK), jnp.float32),
            pltpu.VMEM((UNROLL, BLOCK, SLOTS * BLOCK), jnp.bfloat16),
            pltpu.SemaphoreType.DMA((2, high // CHUNK + 2)),
        ],
        compiler_params=pltpu.CompilerParams(vmem_limit_bytes=24 << 20),
        cost_estimate=pl.CostEstimate(
            flops=4 * pairs * HEAD_DIM, bytes_accessed=8 << 20, transcendentals=pairs
        ),
        name="attend_first" if kept else "attend_rest",
    )(where, rows, own, other, global_own, global_other, *halo)


def swapped(value):
    return lax.ppermute(value, "core", [(0, 1), (1, 0)])


def shards(queries, key_vectors, value_vectors, key_blocks):
    depth = lax.axis_size(Z_AXES)
    breadth = lax.axis_size("y")
    up = [(at, at + 1) for at in range(depth - 1)]
    down = [(at + 1, at) for at in range(depth - 1)]
    where = jnp.stack(
        [lax.axis_index("core"), lax.axis_index(Z_AXES) * PLANE, lax.axis_index("y")]
    )

    received = lax.all_to_all(
        pack(queries, key_vectors, value_vectors), PLANE_AXES, 0, 0, tiled=True
    )

    rows = jnp.stack(
        [key_blocks]
        + [
            lax.ppermute(key_blocks, "y", [(at, (at + step) % breadth) for at in range(breadth)])
            for step in range(1, breadth)
        ]
    )
    above = lax.ppermute(key_blocks[-1, WSEL:], Z_AXES, down)
    own, rows, above = lax.optimization_barrier((received, rows, above))
    other = swapped(own)

    def spread(value, axis):
        copies = jnp.broadcast_to(value[None], (GLOBALS,) + value.shape)
        return lax.all_to_all(copies, axis, 0, 0, tiled=True)

    part = pick_globals(where, rows, above, own)
    held = jnp.sum(lax.all_to_all(part, "near", 0, 0, tiled=True).astype(jnp.float32), axis=0)
    held = lax.psum(held, "far").astype(jnp.bfloat16)
    global_own = spread(held, "near")
    last, global_own = lax.optimization_barrier((own[-WIN // 2 :, :2], global_own))
    pair = (GLOBALS // 2, 2, BLOCK, HEAD_DIM)
    global_own = global_own.reshape(pair)
    global_other = swapped(global_own)
    halo_own = lax.ppermute(last, Z_AXES, up)
    rest = attend(
        WIN // 2, PLANE, where, rows, own, other, global_own, global_other
    )
    rest, halo_own = lax.optimization_barrier((rest, halo_own))
    context = attend(
        0, CHUNK, where, rows, own, other, global_own, global_other,
        halo_own, swapped(halo_own), rest,
    )
    back = lax.all_to_all(context, PLANE_AXES, 0, 0, tiled=True)
    return jnp.transpose(
        back.reshape(HEADS, 2, BLOCK, HEAD_DIM), (1, 2, 0, 3)
    ).reshape(queries.shape)


def solution(mesh):
    fine = Mesh(mesh.devices.reshape(-1, GLOBALS, 4, 4, 2), Z_AXES + PLANE_AXES)
    tokens = P(Z_AXES + PLANE_AXES, None)
    return jax.shard_map(
        shards,
        mesh=fine,
        in_specs=(tokens, tokens, tokens, P(Z_AXES + ("y",), None)),
        out_specs=tokens,
        check_vma=False,
    )
```
